512 devices in a mesh: dp: 64 (over y_hi, z, x), seq: 8 (over y_lo, core).
Axes of the slice: x: 4, y: 8 (y_hi: 2, y_lo: 4; y = y_hi * 4 + y_lo), z: 8, core: 2. Of those that a mesh axis runs over, the one named last changes fastest.
Arguments:
- features: bfloat16 [64, 1024, 768], P('dp', 'seq'), may hold values from -6 to 6
- conv_weight: bfloat16 [5, 768, 1536], P(None, 'dp', 'seq'), as said below
- conv_bias: float32 [1536], replicated, may hold values from -0.5 to 0.5
- norm_gain: float32 [1536], replicated, may hold values from 0.5 to 2
- qkv_weight: bfloat16 [1536, 2560], P('dp', 'seq'), as said below
Outputs:
- mixed: bfloat16 [64, 512, 1536], P('dp', 'seq')
The draws below stay inside these ranges and needn't reach their ends.
Inputs may be any that keep to these rules, and one draw needn't show every extreme that they name: `conv_weight`: entries of order one over the square root of 3840. `qkv_weight`: entries of magnitude at most 10.5 over the square root of 1536.
All inputs are finite; a program needn't handle non-finite values.
Results may differ from the reference program's by a relative error of at most 0.02.
The reference program's roundings to bfloat16 on the way (of `pooled`, `normed`, `qkv`, `probs` and `attended`) count: a program that leaves them out, or rounds other values in their place, can miss the bound.
Values may be sent and summed in bfloat16 or wider, within the bound.
A program may use at most 64 MiB of HBM per device.

```python
import math
import jax
import jax.numpy as jnp
from jax import lax

C_IN = 768
HEADS = 8
HK = 64
HV = 192
KERNEL = 5
D = 1536
BATCH = 64
L_IN = 1024


def draw_conv_weight(key, part):
    shape = (KERNEL, C_IN, D)
    factor = (KERNEL * C_IN) ** (-0.5)
    values = jax.random.truncated_normal(jax.random.fold_in(key, 13), -4.0, 4.0, shape, jnp.float32) * factor
    return values.astype(jnp.bfloat16)


def draw_qkv_weight(key, part):
    width = 2 * HK + HV
    shape = (D, HEADS * width)
    column = jnp.arange(HEADS * width) % width
    is_query_key = column < 2 * HK
    factor = D ** (-0.5)
    entries = jax.random.truncated_normal(jax.random.fold_in(key, 22), -4.0, 4.0, shape, jnp.float32)
    column_scale = jnp.where(is_query_key, 2.0, 1.0)
    return (entries * column_scale[None, :] * factor).astype(jnp.bfloat16)


def steps_of(own_key, shape, split, smallest, largest):
    def one(dim, shards_of):
        steps = jax.random.uniform(jax.random.fold_in(jax.random.fold_in(own_key, 6), dim), (shards_of,), jnp.float32, smallest / len(split), largest / len(split))
        return jnp.repeat(jnp.exp(steps), shape[dim] // shards_of).reshape((-1,) + (1,) * (len(shape) - dim - 1))

    level = one(*split[0])
    for cut in split[1:]:
        level = level * one(*cut)
    return level


def noise(stream_key, dims, deviation, most, pieces=(), held_as=jnp.bfloat16):
    array = jax.random.normal(stream_key, dims, jnp.float32) * deviation
    if len(pieces) > 0:
        array = steps_of(stream_key, dims, pieces, -0.22, 0.18) * array
    return jnp.clip(array, min=-most, max=most).astype(held_as)


def setup_inputs(seed: int = 0) -> dict:
    key_of = jax.random.split(jax.random.key(seed), 6)
    features = noise(key_of[0], (BATCH, L_IN, C_IN), 1.0, 6.0, ((0, 64), (1, 8)))
    conv_weight = draw_conv_weight(jax.random.fold_in(key_of[5], 71), 0)
    conv_bias = jnp.clip(jax.random.uniform(key_of[2], (D,), jnp.float32, -0.5, 0.5), -0.5, 0.5)
    norm_gain = jnp.clip(jnp.exp(jax.random.uniform(key_of[3], (D,), jnp.float32, math.log(0.5), math.log(2.0))), 0.5, 2.0)
    qkv_weight = draw_qkv_weight(jax.random.fold_in(key_of[5], 71), 0)
    return {"features": features, "conv_weight": conv_weight, "conv_bias": conv_bias, "norm_gain": norm_gain, "qkv_weight": qkv_weight}


def attend(query, keys, values):
    length = query.shape[0]
    block = min(512, length)
    scale = HK ** (-0.5)
    blocks = query.reshape(length // block, block, query.shape[1])

    def one_block(rows):
        scores = jnp.dot(rows, keys.T, preferred_element_type=jnp.float32) * scale
        top = lax.optimization_barrier(jnp.max(scores, axis=-1, keepdims=True))
        expo = jnp.exp(scores - top)
        probs = (expo / lax.optimization_barrier(jnp.sum(expo, axis=-1, keepdims=True))).astype(jnp.bfloat16)
        return jnp.dot(probs, values, preferred_element_type=jnp.float32).astype(jnp.bfloat16)
    return lax.map(one_block, blocks).reshape(length, values.shape[1])

def reference(features, conv_weight, conv_bias, norm_gain, qkv_weight):
    half = KERNEL // 2
    width = 2 * HK + HV

    def one_sequence(seq_in):
        rows = seq_in.shape[0]
        padded = jnp.pad(seq_in, ((half, half), (0, 0)))
        conv_out = jnp.zeros((rows, D), jnp.float32)
        for tap in range(KERNEL):
            conv_out = conv_out + jnp.dot(padded[tap:tap + rows], conv_weight[tap], preferred_element_type=jnp.float32)
        conv_out = conv_out + conv_bias
        active = jax.nn.gelu(conv_out, approximate=True)
        pooled = lax.optimization_barrier(jnp.max(active.reshape(rows // 2, 2, D), axis=1)).astype(jnp.bfloat16)
        values32 = pooled.astype(jnp.float32)
        mean = lax.optimization_barrier(jnp.mean(values32, axis=-1, keepdims=True))
        centred = values32 - mean
        var = lax.optimization_barrier(jnp.mean(centred * centred, axis=-1, keepdims=True))
        normed = (centred / jnp.sqrt(var + 1e-05) * norm_gain).astype(jnp.bfloat16)
        qkv = jnp.dot(normed, qkv_weight, preferred_element_type=jnp.float32).astype(jnp.bfloat16)
        outputs = []
        for head in range(HEADS):
            start = head * width
            outputs.append(attend(qkv[:, start:start + HK], qkv[:, start + HK:start + 2 * HK], qkv[:, start + 2 * HK:start + width]))
        attended = jnp.concatenate(outputs, axis=1)
        return (pooled.astype(jnp.float32) + attended.astype(jnp.float32)).astype(jnp.bfloat16)
    return lax.map(one_sequence, features)
```

```python
import jax
import jax.numpy as jnp
from jax import lax
from jax.sharding import PartitionSpec as P

HK = 64
HV = 192


def attend(query, keys, values):
    scale = query.shape[1] ** (-0.5)
    scores = jnp.dot(query, keys.T, preferred_element_type=jnp.float32) * scale
    top = jnp.max(scores, axis=-1, keepdims=True)
    expo = jnp.exp(scores - top)
    probs = (expo / jnp.sum(expo, axis=-1, keepdims=True)).astype(jnp.bfloat16)
    return jnp.dot(probs, values, preferred_element_type=jnp.float32).astype(jnp.bfloat16)


def shards(features, conv_weight, conv_bias, norm_gain, qkv_weight):
    taps, _, cols = conv_weight.shape
    half = taps // 2
    weight = lax.all_gather(conv_weight, "dp", axis=1, tiled=True)
    seq_in = lax.all_gather(features[0], "seq", axis=0, tiled=True)
    projection = lax.all_gather(qkv_weight, "dp", axis=0, tiled=True)
    rows = seq_in.shape[0]
    padded = jnp.pad(seq_in, ((half, half), (0, 0)))
    total = jnp.zeros((rows, cols), jnp.float32)
    for tap in range(taps):
        total = total + jnp.dot(padded[tap : tap + rows], weight[tap], preferred_element_type=jnp.float32)
    mine = lax.axis_index("seq") * cols
    total = total + lax.dynamic_slice_in_dim(conv_bias, mine, cols)
    active = jax.nn.gelu(total, approximate=True)
    pooled = jnp.max(active.reshape(rows // 2, 2, cols), axis=1).astype(jnp.bfloat16)
    whole = lax.all_gather(pooled, "seq", axis=1, tiled=True)
    values32 = whole.astype(jnp.float32)
    mean = jnp.mean(values32, axis=-1, keepdims=True)
    centred = values32 - mean
    var = jnp.mean(centred * centred, axis=-1, keepdims=True)
    normed = (centred / jnp.sqrt(var + 1e-05) * norm_gain).astype(jnp.bfloat16)
    qkv = jnp.dot(normed, projection, preferred_element_type=jnp.float32).astype(jnp.bfloat16)
    width = 2 * HK + HV
    outputs = attend(qkv[:, 0:HK], qkv[:, HK : 2 * HK], qkv[:, 2 * HK : width])
    mixed = (pooled.astype(jnp.float32) + outputs.astype(jnp.float32)).astype(jnp.bfloat16)
    arrived = lax.all_to_all(mixed, "seq", split_axis=0, concat_axis=1, tiled=True)
    return arrived[None]


def solution(mesh):
    return jax.shard_map(
        shards,
        mesh=mesh,
        in_specs=(P("dp", "seq", None), P(None, "dp", "seq"), P(), P(), P("dp", "seq")),
        out_specs=P("dp", "seq", None),
        check_vma=False,
    )
```

```python
import functools

import jax
import jax.numpy as jnp
from jax import lax
from jax.experimental import pallas as pl
from jax.experimental.pallas import tpu as pltpu
from jax.sharding import PartitionSpec as P

HK = 64
HV = 192
NH = 2
NX = 4
BF = jnp.bfloat16
F32 = jnp.float32


def kernel(
    nz, nx, ny,
    feat_ref, conv_ref, bias_ref, gain_ref, proj_ref, out_ref,
    feat, edge, edges, ext, prev, later,
    w0, w1, wbuild, wc, p0, p1, pbuild, pw,
    pool, qkv, mixed, landed,
    send_sems, r_feat, r_edge, r_w0, r_p0, r_w1, r_p1,
    r_wup, r_wdown, r_wsib, r_pup, r_pdown, r_psib, r_pool, r_kv, r_mix,
):
    dp, seq = lax.axis_index("dp"), lax.axis_index("seq")
    h, z, x = lax.div(dp, nz * nx), lax.rem(lax.div(dp, nx), nz), lax.rem(dp, nx)
    y, c = lax.div(seq, 2), lax.rem(seq, 2)

    def at(hh, zz, xx, yy, cc):
        return ((hh * nz + zz) * nx + xx, yy * 2 + cc)

    sibling = at(h, z, x, y, 1 - c)
    above = at(h, lax.rem(z + 1, nz), x, y, c)
    below = at(h, lax.rem(z + nz - 1, nz), x, y, c)
    others_y = [lax.rem(y + d, ny) for d in range(1, ny)]
    others_x = [lax.rem(x + d, nx) for d in range(1, nx)]

    partners = [sibling, above, below, at(1 - h, z, x, y, 0), at(1 - h, z, x, y, 1)]
    partners += [at(h, z, x, yy, c) for yy in others_y]
    partners += [at(h, z, x, yy, 1 - c) for yy in others_y]
    partners += [at(h, z, xx, y, c) for xx in others_x]
    barrier = pltpu.get_barrier_semaphore()
    for device in partners:
        pl.semaphore_signal(barrier, inc=1, device_id=device, device_id_type=pl.DeviceIdType.MESH)
    pl.semaphore_wait(barrier, len(partners))

    pending = []

    def copy(src, dst, recv, device, index):
        return pltpu.make_async_remote_copy(
            src_ref=src, dst_ref=dst, send_sem=send_sems.at[index], recv_sem=recv,
            device_id=device, device_id_type=pl.DeviceIdType.MESH,
        )

    def send(src, dst, recv, device):
        cp = copy(src, dst, recv, device, len(pending))
        cp.start()
        pending.append(cp)

    def arrived(dst, recv):
        copy(dst, dst, recv, sibling, 0).wait_recv()

    rows = conv_ref.shape[1]
    send(conv_ref, w0.at[c], r_w0.at[c], at(1 - h, z, x, y, h))
    send(proj_ref, p0.at[c], r_p0.at[c], at(1 - h, z, x, y, h))
    extra = [
        copy(conv_ref, w0.at[c], r_w0.at[c], sibling, len(pending)),
        copy(proj_ref, p0.at[c], r_p0.at[c], sibling, len(pending) + 1),
    ]
    own = c == h

    @pl.when(jnp.logical_not(own))
    def _():
        for cp in extra:
            cp.start()

    used = len(pending) + 2
    pending.extend([None, None])

    @pl.when(own)
    def _():
        w0[c] = conv_ref[...]
        p0[c] = proj_ref[...]

    half_rows = feat_ref.shape[0]
    first = feat_ref[0:16, :].astype(F32)[0:1]
    last = feat_ref[half_rows - 16 : half_rows, :].astype(F32)[15:16]
    edge[...] = jnp.concatenate([first, last], axis=0).astype(BF)
    feat[y] = feat_ref[...]
    for yy in others_y:
        send(edge, edges.at[1 + y], r_edge.at[y], at(h, z, x, yy, 1 - c))
    send(edge, edges.at[1 + y], r_edge.at[y], sibling)
    for yy in others_y:
        send(feat_ref, feat.at[y], r_feat.at[y], at(h, z, x, yy, c))
    zero = jnp.zeros(edge.shape, BF)
    edges[0] = zero
    edges[ny + 1] = zero

    arrived(w0.at[1 - c], r_w0.at[1 - c])

    @pl.when(jnp.logical_not(own))
    def _():
        arrived(w0.at[c], r_w0.at[c])

    w1[x] = jnp.concatenate([w0[0].astype(F32), w0[1].astype(F32)], axis=2).astype(BF)
    for xx in others_x:
        send(w1.at[x], w1.at[x], r_w1.at[x], at(h, z, xx, y, c))

    arrived(p0.at[1 - c], r_p0.at[1 - c])

    @pl.when(jnp.logical_not(own))
    def _():
        arrived(p0.at[c], r_p0.at[c])

    a, b = p0[0].astype(F32), p0[1].astype(F32)
    p1[x] = jnp.concatenate(
        [a[:, :HK], b[:, :HK], a[:, HK : 2 * HK], b[:, HK : 2 * HK], a[:, 2 * HK :], b[:, 2 * HK :]],
        axis=1,
    ).astype(BF)
    for xx in others_x:
        send(p1.at[x], p1.at[x], r_p1.at[x], at(h, z, xx, y, c))

    taps = conv_ref.shape[0]
    w_rows = rows * nx
    p_rows = proj_ref.shape[0] * nx

    def w_block(cc, zz):
        return wc.at[:, pl.ds(pl.multiple_of((cc * nz + zz) * w_rows, 16), w_rows), :]

    def p_block(cc, zz):
        return pw.at[pl.ds(pl.multiple_of((cc * nz + zz) * p_rows, 16), p_rows), :]

    ups, downs = nz // 2, nz - 1 - nz // 2

    def ring(block, r_up, r_down, r_sib):
        mine = block(c, z)
        send(mine, mine, r_up.at[0], above)
        if downs:
            send(mine, mine, r_down.at[0], below)
        send(mine, mine, r_sib.at[0], sibling)
        for d in range(ups):
            got = block(c, lax.rem(z - 1 - d + nz, nz))
            arrived(got, r_up.at[d])
            if d + 1 < ups:
                send(got, got, r_up.at[d + 1], above)
            send(got, got, r_sib.at[1 + d], sibling)
            if d < downs:
                got = block(c, lax.rem(z + 1 + d, nz))
                arrived(got, r_down.at[d])
                if d + 1 < downs:
                    send(got, got, r_down.at[d + 1], below)
                send(got, got, r_sib.at[1 + ups + d], sibling)
            yield d

    def from_sibling(block, r_sib):
        zs = [z] + [lax.rem(z - 1 - d + nz, nz) for d in range(ups)] + [lax.rem(z + 1 + d, nz) for d in range(downs)]
        for k, zz in enumerate(zs):
            arrived(block(1 - c, zz), r_sib.at[k])

    for xx in others_x:
        arrived(w1.at[xx], r_w1.at[xx])
    for t in range(taps):
        for xx in range(nx):
            wbuild[t, rows * xx : rows * (xx + 1), :] = w1[xx, t].astype(F32)
    w_mine = pl.multiple_of((c * nz + z) * w_rows, 16)
    for t in range(taps):
        wc[t, pl.ds(w_mine, w_rows), :] = wbuild[t].astype(BF)

    def shifted(yy):
        ext[8 : 8 + half_rows, :] = feat[yy].astype(F32)
        before = edges[yy + c].astype(F32)
        after = edges[yy + c + 1].astype(F32)
        ext[7:8, :] = before[1:2]
        ext[8 + half_rows : 9 + half_rows, :] = after[0:1]
        prev[yy] = ext[7 : 7 + half_rows, :].astype(BF)
        later[yy] = ext[9 : 9 + half_rows, :].astype(BF)

    conv_ring = ring(w_block, r_wup, r_wdown, r_wsib)
    done = 0
    for d in conv_ring:
        if d == 0:
            for xx in others_x:
                arrived(p1.at[xx], r_p1.at[xx])
            step = proj_ref.shape[0]
            for xx in range(nx):
                pbuild[step * xx : step * (xx + 1), :] = p1[xx].astype(F32)
            pw[pl.ds(pl.multiple_of((c * nz + z) * p_rows, 16), p_rows), :] = pbuild[...].astype(BF)
        if d == ups - 1:
            for yy in others_y:
                arrived(edges.at[1 + yy], r_edge.at[yy])
            arrived(edges.at[1 + y], r_edge.at[y])
            for yy in others_y:
                arrived(feat.at[yy], r_feat.at[yy])
            for yy in range(ny):
                shifted(yy)
    from_sibling(w_block, r_wsib)

    cin = wc.shape[1]
    cols = wc.shape[2]
    bias = bias_ref[:, pl.ds(pl.multiple_of(y * cols, 128), cols)]
    wflat = wc.reshape(taps * cin, cols)

    def dot(left, right):
        return jnp.dot(left, right, preferred_element_type=F32)

    def gelu(value):
        value = value + bias
        inner = 0.7978845608028654 * (value + 0.044715 * (value * value * value))
        return value * (0.5 * (1.0 + jnp.tanh(inner)))

    for yy in range(ny):
        before, now, after = prev[yy], feat[yy], later[yy]
        even = dot(before, wflat[0 : 2 * cin, :]) + dot(now, wflat[2 * cin : 4 * cin, :])
        even = even + dot(after[:, :cin], wflat[4 * cin :, :])
        odd = dot(before[:, cin:], wflat[0:cin, :]) + dot(now, wflat[cin : 3 * cin, :])
        odd = odd + dot(after, wflat[3 * cin :, :])
        pool[y, yy * half_rows : (yy + 1) * half_rows, :] = jnp.maximum(gelu(even), gelu(odd)).astype(BF)
    for yy in others_y:
        send(pool.at[y], pool.at[y], r_pool.at[y], at(h, z, x, yy, c))

    for _ in ring(p_block, r_pup, r_pdown, r_psib):
        pass
    from_sibling(p_block, r_psib)

    for yy in others_y:
        arrived(pool.at[yy], r_pool.at[yy])
    width = ny * cols
    total = functools.reduce(
        jnp.add, [jnp.sum(pool[yy].astype(F32), axis=1, keepdims=True) for yy in range(ny)]
    )
    mean = total * (1.0 / width)
    square = functools.reduce(
        jnp.add, [jnp.sum(jnp.square(pool[yy].astype(F32) - mean), axis=1, keepdims=True) for yy in range(ny)]
    )
    inverse = 1.0 / jnp.sqrt(square * (1.0 / width) + 1e-05)
    acc = None
    for yy in range(ny):
        normed = ((pool[yy].astype(F32) - mean) * inverse * gain_ref[:, yy * cols : (yy + 1) * cols]).astype(BF)
        part = dot(normed, pw[yy * cols : (yy + 1) * cols, :])
        acc = part if acc is None else acc + part
    qkv[c] = acc.astype(BF)
    send(qkv.at[c], qkv.at[c], r_kv.at[c], sibling)
    arrived(qkv.at[1 - c], r_kv.at[1 - c])

    query = qkv[c, :, : 2 * HK]
    lane = lax.broadcasted_iota(jnp.int32, query.shape, 1)
    outs = []
    for head in range(2):
        q = jnp.where((lane < HK) if head == 0 else (lane >= HK), query, jnp.zeros_like(query))
        scores = [
            lax.dot_general(q, qkv[k, :, 2 * HK : 4 * HK], (((1,), (1,)), ((), ())), preferred_element_type=F32)
            * (HK ** -0.5)
            for k in range(2)
        ]
        top = jnp.maximum(*[jnp.max(s, axis=1, keepdims=True) for s in scores])
        expo = [jnp.exp(s - top) for s in scores]
        inv = 1.0 / (jnp.sum(expo[0], axis=1, keepdims=True) + jnp.sum(expo[1], axis=1, keepdims=True))
        probs = [(e * inv).astype(BF) for e in expo]
        outs.append(dot(probs[0], qkv[0, :, 4 * HK :]) + dot(probs[1], qkv[1, :, 4 * HK :]))
    lane = lax.broadcasted_iota(jnp.int32, outs[0].shape, 1)
    attended = jnp.where(lane < HV, outs[0], outs[1]).astype(BF)
    mixed[...] = (pool[y].astype(F32) + attended.astype(F32)).astype(BF).reshape(mixed.shape)

    for yy in others_y:
        send(mixed.at[yy], landed.at[y], r_mix.at[y], at(h, z, x, yy, c))
    landed[y] = mixed[y]
    for yy in others_y:
        arrived(landed.at[yy], r_mix.at[yy])
    for yy in range(ny):
        out_ref[:, yy * cols : (yy + 1) * cols] = landed[yy]

    for cp in pending:
        if cp is not None:
            cp.wait_send()

    @pl.when(jnp.logical_not(own))
    def _():
        for cp in extra:
            cp.wait_send()


def shards(features, conv_weight, conv_bias, norm_gain, qkv_weight):
    dp, ny = lax.axis_size("dp"), lax.axis_size("seq") // 2
    nx, nz = NX, dp // (NH * NX)
    taps, rows, cols = conv_weight.shape
    cols, cin, width = 2 * cols, rows * dp, 2 * ny * cols
    half_rows = features.shape[1] // 2
    step, heads = qkv_weight.shape
    heads = 2 * heads
    positions = half_rows * ny
    dma = pltpu.SemaphoreType.DMA
    vmem = pltpu.VMEM
    ups, downs = nz // 2, nz - 1 - nz // 2
    sends = 4 + ny + (ny - 1) + 2 * (nx - 1) + 2 * (2 * nz - 1) + (ny - 1) + 1 + (ny - 1)
    scratch = [
        vmem((ny, half_rows, 2 * cin), BF),
        vmem((2, 2 * cin), BF),
        vmem((ny + 2, 2, 2 * cin), BF),
        vmem((half_rows + 16, 2 * cin), F32),
        vmem((ny, half_rows, 2 * cin), BF),
        vmem((ny, half_rows, 2 * cin), BF),
        vmem((2,) + conv_weight.shape, BF),
        vmem((nx, taps, rows, cols), BF),
        vmem((taps, nx * rows, cols), F32),
        vmem((taps, cin, cols), BF),
        vmem((2,) + qkv_weight.shape, BF),
        vmem((nx, step, heads), BF),
        vmem((nx * step, heads), F32),
        vmem((width, heads), BF),
        vmem((ny, positions, cols), BF),
        vmem((2, positions, heads), BF),
        vmem((ny, half_rows, cols), BF),
        vmem((ny, half_rows, cols), BF),
        dma((sends,)), dma((ny,)), dma((ny,)), dma((2,)), dma((2,)), dma((nx,)), dma((nx,)),
        dma((ups,)), dma((max(downs, 1),)), dma((nz,)),
        dma((ups,)), dma((max(downs, 1),)), dma((nz,)),
        dma((ny,)), dma((2,)), dma((ny,)),
    ]
    out = pl.pallas_call(
        functools.partial(kernel, nz, nx, ny),
        out_shape=jax.ShapeDtypeStruct((half_rows, width), BF),
        in_specs=[pl.BlockSpec(memory_space=pltpu.VMEM)] * 5,
        out_specs=pl.BlockSpec(memory_space=pltpu.VMEM),
        scratch_shapes=scratch,
        compiler_params=pltpu.CompilerParams(
            collective_id=0, has_side_effects=True, vmem_limit_bytes=48 * 2**20
        ),
        name="section",
    )(
        features[0].reshape(half_rows, 2 * cin),
        conv_weight,
        conv_bias.reshape(1, width),
        norm_gain.reshape(1, width),
        qkv_weight,
    )
    return out[None]


def solution(mesh):
    return jax.shard_map(
        shards,
        mesh=mesh,
        in_specs=(P("dp", "seq", None), P(None, "dp", "seq"), P(), P(), P("dp", "seq")),
        out_specs=P("dp", "seq", None),
        check_vma=False,
    )
```

```python
import functools

import jax
import jax.numpy as jnp
from jax import lax
from jax.experimental import pallas as pl
from jax.experimental.pallas import tpu as pltpu
from jax.sharding import PartitionSpec as P

HK = 64
HV = 192
NH = 2
NX = 4
BF = jnp.bfloat16
F32 = jnp.float32
P_START = 3
PARTS = ((0, 2), (2, 2), (4, 1))


def kernel(
    nz, nx, ny,
    feat_in, conv_in, bias_in, gain_in, proj_in, out_ref,
    feat_ref, conv_ref, bias_ref, gain_ref, proj_ref,
    mine, feat, edge, edges, ext, wide, prev, later,
    wpack, wown, w0, w1, wflat32, wbuild, wc, pown, p0, p1, pbuild, pw,
    pool, qkv, mixed, landed,
    in_sems, send_sems, r_feat, r_edge, r_w0, r_p0, r_w1, r_p1,
    r_wa, r_wb, r_wsib, r_pup, r_pdown, r_psib, r_pool, r_kv, r_mix,
):
    dp, seq = lax.axis_index("dp"), lax.axis_index("seq")
    h, z, x = lax.div(dp, nz * nx), lax.rem(lax.div(dp, nx), nz), lax.rem(dp, nx)
    y, c = lax.div(seq, 2), lax.rem(seq, 2)
    turn = 1 - 2 * c

    def at(hh, zz, xx, yy, cc):
        return ((hh * nz + zz) * nx + xx, yy * 2 + cc)

    def round_z(offset):
        return lax.rem(z + offset + 2 * nz, nz)

    def round_x(offset):
        return lax.rem(x + offset + nx, nx)

    sibling = at(h, z, x, y, 1 - c)
    z_next, z_last = at(h, round_z(turn), x, y, c), at(h, round_z(-turn), x, y, c)
    x_next, x_last = at(h, z, round_x(turn), y, c), at(h, z, round_x(-turn), y, c)
    others_y = [lax.rem(y + d, ny) for d in (2, 1, 3)]
    others_x = [lax.rem(x + d, nx) for d in range(1, nx)]

    partners = [sibling, z_next, z_last, at(1 - h, z, x, y, 0), at(1 - h, z, x, y, 1)]
    partners += [at(h, z, x, yy, c) for yy in others_y]
    partners += [at(h, z, x, yy, 1 - c) for yy in others_y]
    partners += [at(h, z, xx, y, c) for xx in others_x]
    inputs = ((conv_in, conv_ref), (feat_in, feat_ref), (proj_in, proj_ref), (bias_in, bias_ref), (gain_in, gain_ref))
    loads = [pltpu.make_async_copy(src, dst, in_sems.at[i]) for i, (src, dst) in enumerate(inputs)]
    for load in loads:
        load.start()
    barrier = pltpu.get_barrier_semaphore()
    for device in partners:
        pl.semaphore_signal(barrier, inc=1, device_id=device, device_id_type=pl.DeviceIdType.MESH)

    for load in loads:
        load.wait()

    half_rows, lanes = mine.shape
    cin = lanes // 2
    for k in range(cin // 128):
        ext[k] = feat_ref[:, 128 * k : 128 * (k + 1)].astype(F32)
        mine[:, 128 * k : 128 * (k + 1)] = ext[k, pl.ds(0, half_rows, stride=2), :].astype(BF)
        mine[:, cin + 128 * k : cin + 128 * (k + 1)] = ext[k, pl.ds(1, half_rows, stride=2), :].astype(BF)
    first = mine[0:16, :].astype(F32)[0:1]
    last = mine[half_rows - 16 :, :].astype(F32)[15:16]
    strips = [row[:, 128 * k : 128 * (k + 1)] for row in (first, last) for k in range(lanes // 128)]
    spare = edge.shape[0] - len(strips)
    edge[...] = jnp.concatenate(strips + [jnp.zeros((spare, 128), F32)], axis=0).astype(BF)
    zero = jnp.zeros(edge.shape, BF)
    edges[0] = zero
    edges[ny + 1] = zero
    own = c == h
    taps, rows, cols = conv_ref.shape
    p_in, p_cols = proj_ref.shape
    wpack[...] = jnp.zeros(wpack.shape, F32)
    for t in range(taps):
        wpack[rows * t : rows * (t + 1), :cols] = conv_ref[t].astype(F32)
    wown[...] = wpack[...].astype(BF)
    pown[...] = jnp.zeros(pown.shape, BF)
    pown[:p_in, :p_cols] = proj_ref[...]

    @pl.when(own)
    def _():
        w0[c] = wown[...]
        p0[c] = pown[...]

    pl.semaphore_wait(barrier, len(partners))

    pending = []

    def copy(src, dst, recv, device, index):
        return pltpu.make_async_remote_copy(
            src_ref=src, dst_ref=dst, send_sem=send_sems.at[index], recv_sem=recv,
            device_id=device, device_id_type=pl.DeviceIdType.MESH,
        )

    def send(src, dst, recv, device, when=None):
        cp = copy(src, dst, recv, device, len(pending))
        if when is None:
            cp.start()
        else:
            pl.when(when)(cp.start)
        pending.append((cp, when))

    def arrived(dst, recv):
        copy(dst, dst, recv, sibling, 0).wait_recv()

    middle = jnp.logical_or(y == 1, y == 2)
    pass_from, pass_to = jnp.where(y == 1, 3, 0), jnp.where(y == 1, 0, 3)

    def spread(ref, dst, recv):
        for yy in others_y:
            send(ref, dst, recv.at[y], at(h, z, x, yy, c), jnp.abs(yy - y) < 3)

    def pass_on(block, recv):
        @pl.when(middle)
        def _():
            arrived(block(pass_from), recv.at[pass_from])

        send(block(pass_from), block(pass_from), recv.at[pass_from], at(h, z, x, pass_to, c), middle)

    def rest(block, recv):
        for yy in others_y:
            @pl.when(jnp.logical_not(jnp.logical_and(middle, yy == pass_from)))
            def _():
                arrived(block(yy), recv.at[yy])

    other = jnp.logical_not(own)
    send(wown, w0.at[c], r_w0.at[c], at(1 - h, z, x, y, h))
    send(wown, w0.at[c], r_w0.at[c], sibling, other)

    feat[y] = mine[...]
    spread(mine, feat.at[y], r_feat)
    for yy in others_y:
        send(edge, edges.at[1 + y], r_edge.at[y], at(h, z, x, yy, 1 - c))
    send(edge, edges.at[1 + y], r_edge.at[y], sibling)
    send(pown, p0.at[c], r_p0.at[c], at(1 - h, z, x, y, h))
    send(pown, p0.at[c], r_p0.at[c], sibling, other)

    arrived(w0.at[1 - c], r_w0.at[1 - c])

    @pl.when(other)
    def _():
        arrived(w0.at[c], r_w0.at[c])

    w1[x] = jnp.concatenate([w0[0].astype(F32)[:, :cols], w0[1].astype(F32)[:, :cols]], axis=1).astype(BF)
    for xx in others_x:
        send(w1.at[x], w1.at[x], r_w1.at[x], at(h, z, xx, y, c))

    w_rows = rows * nx
    p_rows = p_in * nx
    ups, downs = nz // 2, nz - 1 - nz // 2
    count = len(PARTS)

    def carried(distance):
        return lax.rem(z + x + c + distance, 2) == 0

    def p_block(cc, zz):
        return pw.at[pl.ds(pl.multiple_of((cc * nz + zz) * p_rows, 16), p_rows), :]

    for xx in others_x:
        arrived(w1.at[xx], r_w1.at[xx])
    for xx in range(nx):
        wflat32[...] = w1[xx].astype(F32)
        for t in range(taps):
            wbuild[t, rows * xx : rows * (xx + 1), :] = wflat32[rows * t : rows * (t + 1), :]
    wc[c * nz + z] = wbuild[...].astype(BF)

    def w_block(j, cc, zz):
        tap, size = PARTS[j]
        return wc.at[cc * nz + zz, tap : tap + size]

    to_sibling = {}

    def w_start(j):
        block = w_block(j, c, z)
        send(block, block, r_wa.at[j, 0], z_next, carried(0))
        if downs:
            send(block, block, r_wb.at[j, 0], z_last, carried(0))
        send(block, block, r_wsib.at[j, 0], sibling)

    def ways(d):
        found = [(round_z(-turn * (1 + d)), r_wa, ups, z_next, x_next, 1 + d)]
        if d < downs:
            found.append((round_z(turn * (1 + d)), r_wb, downs, z_last, x_last, 1 + ups + d))
        return found

    def w_step(j, d):
        for zz, recv, steps, z_to, x_to, k in ways(d):
            block = w_block(j, c, zz)

            @pl.when(carried(1 + d))
            def _():
                arrived(block, recv.at[j, d])

            if d + 1 < steps:
                send(block, block, recv.at[j, d + 1], z_to, carried(1 + d))
            send(block, block, recv.at[j, d], x_to, carried(1 + d))
            cp = copy(block, block, r_wsib.at[j, k], sibling, len(pending))
            pl.when(carried(1 + d))(cp.start)
            pending.append((cp, None))
            to_sibling[j, k] = cp

    def w_finish(j, d):
        for zz, recv, steps, z_to, x_to, k in ways(d):
            @pl.when(carried(d))
            def _():
                arrived(w_block(j, c, zz), recv.at[j, d])
                to_sibling[j, k].start()

    def w_sibling(j):
        zs = [z] + [round_z(turn * (1 + d)) for d in range(ups)] + [round_z(-turn * (1 + d)) for d in range(downs)]
        for k, zz in enumerate(zs):
            arrived(w_block(j, 1 - c, zz), r_wsib.at[j, k])

    def p_join():
        arrived(p0.at[1 - c], r_p0.at[1 - c])

        @pl.when(other)
        def _():
            arrived(p0.at[c], r_p0.at[c])

        a, b = p0[0].astype(F32)[:, :p_cols], p0[1].astype(F32)[:, :p_cols]
        p1[x] = jnp.concatenate(
            [a[:, :HK], b[:, :HK], a[:, HK : 2 * HK], b[:, HK : 2 * HK], a[:, 2 * HK :], b[:, 2 * HK :]],
            axis=1,
        ).astype(BF)
        for xx in others_x:
            send(p1.at[x], p1.at[x], r_p1.at[x], at(h, z, xx, y, c))

    def p_start():
        for xx in others_x:
            arrived(p1.at[xx], r_p1.at[xx])
        for xx in range(nx):
            pbuild[p_in * xx : p_in * (xx + 1), :] = p1[xx].astype(F32)[:p_in]
        pw[pl.ds(pl.multiple_of((c * nz + z) * p_rows, 16), p_rows), :] = pbuild[...].astype(BF)
        block = p_block(c, z)
        send(block, block, r_pup.at[0], z_next)
        if downs:
            send(block, block, r_pdown.at[0], z_last)
        send(block, block, r_psib.at[0], sibling)

    def p_step(d):
        got = p_block(c, round_z(-turn * (1 + d)))
        arrived(got, r_pup.at[d])
        if d + 1 < ups:
            send(got, got, r_pup.at[d + 1], z_next)
        send(got, got, r_psib.at[1 + d], sibling)
        if d < downs:
            got = p_block(c, round_z(turn * (1 + d)))
            arrived(got, r_pdown.at[d])
            if d + 1 < downs:
                send(got, got, r_pdown.at[d + 1], z_last)
            send(got, got, r_psib.at[1 + ups + d], sibling)

    def p_sibling():
        zs = [z] + [round_z(turn * (1 + d)) for d in range(ups)] + [round_z(-turn * (1 + d)) for d in range(downs)]
        for k, zz in enumerate(zs):
            arrived(p_block(1 - c, zz), r_psib.at[k])

    def conv_inputs():
        for yy in others_y:
            arrived(edges.at[1 + yy], r_edge.at[yy])
        arrived(edges.at[1 + y], r_edge.at[y])
        rest(lambda yy: feat.at[yy], r_feat)
        for yy in range(ny):
            wide[8 : 8 + half_rows, :] = feat[yy].astype(F32)
            before, after = edges[yy + c].astype(F32), edges[yy + c + 1].astype(F32)
            for k in range(lanes // 128):
                wide[7:8, 128 * k : 128 * (k + 1)] = before[lanes // 128 + k : lanes // 128 + k + 1]
                wide[8 + half_rows : 9 + half_rows, 128 * k : 128 * (k + 1)] = after[k : k + 1]
            prev[yy] = wide[7 : 7 + half_rows, :].astype(BF)
            later[yy] = wide[9 : 9 + half_rows, :].astype(BF)

    for t in range(ups + 2):
        for j in range(count):
            if t == 0:
                w_start(j)
            if 0 < t <= ups:
                w_step(j, t - 1)
            if 1 < t:
                w_finish(j, t - 2)
        if t == 0:
            p_join()
        if t == 1:
            pass_on(lambda yy: feat.at[yy], r_feat)
        if t == P_START:
            p_start()
        if t > P_START:
            p_step(t - P_START - 1)
        if t == ups - 1:
            conv_inputs()

    cols = wc.shape[3]

    def dot(left, right):
        return jnp.dot(left, right, preferred_element_type=F32)

    def gelu(value, bias):
        value = value + bias
        inner = 0.7978845608028654 * (value + 0.044715 * (value * value * value))
        return value * (0.5 * (1.0 + jnp.tanh(inner)))

    def pool_part(part):
        return lambda yy: pool.at[yy, 2 * half_rows * part : 2 * half_rows * (part + 1)]

    def conv(part):
        def weight(first, last):
            return jnp.concatenate([wc[:, t].reshape(cin, cols) for t in range(first, last)], axis=0)

        bias = jnp.concatenate([bias_ref[pl.ds(y * (cols // 128) + k, 1), :] for k in range(cols // 128)], axis=1)
        yy = 2 * part

        def pair(ref):
            return ref[yy : yy + 2].reshape(2 * half_rows, lanes)

        before, now, after = pair(prev), pair(feat), pair(later)
        even = dot(before, weight(0, 2)) + dot(now, weight(2, 4)) + dot(after[:, :cin], weight(4, 5))
        odd = dot(before[:, cin:], weight(0, 1)) + dot(now, weight(1, 3)) + dot(after, weight(3, 5))
        value = jnp.maximum(gelu(even, bias), gelu(odd, bias)).astype(BF)
        pool[y, yy * half_rows : (yy + 2) * half_rows, :] = value

    for j in range(count):
        w_sibling(j)
    for part in range(ny // 2):
        conv(part)
        spread(pool_part(part)(y), pool_part(part)(y), r_pool.at[part])
    left = list(range(ups + 1 - P_START, ups))
    for part in range(ny // 2):
        pass_on(pool_part(part), r_pool.at[part])
        if left:
            p_step(left.pop(0))
    for d in left:
        p_step(d)
    p_sibling()

    for part in range(ny // 2):
        rest(pool_part(part), r_pool.at[part])
    width = ny * cols
    total = functools.reduce(
        jnp.add, [jnp.sum(pool[yy].astype(F32), axis=1, keepdims=True) for yy in range(ny)]
    )
    mean = total * (1.0 / width)
    square = functools.reduce(
        jnp.add, [jnp.sum(jnp.square(pool[yy].astype(F32) - mean), axis=1, keepdims=True) for yy in range(ny)]
    )
    inverse = 1.0 / jnp.sqrt(square * (1.0 / width) + 1e-05)

    def gain(yy):
        k = cols // 128
        return jnp.concatenate([gain_ref[yy * k + i : yy * k + i + 1, :] for i in range(k)], axis=1)

    acc = None
    for yy in range(ny):
        normed = ((pool[yy].astype(F32) - mean) * inverse * gain(yy)).astype(BF)
        part = dot(normed, pw[yy * cols : (yy + 1) * cols, :])
        acc = part if acc is None else acc + part
    qkv[c] = acc.astype(BF)
    send(qkv.at[c], qkv.at[c], r_kv.at[c], sibling)

    half = half_rows * ny // 2
    lane = lax.broadcasted_iota(jnp.int32, (half, 2 * HK), 1)
    wide_lane = lax.broadcasted_iota(jnp.int32, (half, cols), 1)

    def attend(side, first):
        rows_here = pl.ds(pl.multiple_of(side * half, half), half)
        query = qkv[c, rows_here, : 2 * HK]
        none = jnp.zeros_like(query)
        both = jnp.concatenate([jnp.where(lane < HK, query, none), jnp.where(lane < HK, none, query)], axis=0)

        def score(core):
            keys = qkv[core, :, 2 * HK : 4 * HK]
            return lax.dot_general(both, keys, (((1,), (1,)), ((), ())), preferred_element_type=F32) * (HK ** -0.5)

        here = score(c)
        if first:
            arrived(qkv.at[1 - c], r_kv.at[1 - c])
        there = score(1 - c)
        top = jnp.maximum(jnp.max(here, axis=1, keepdims=True), jnp.max(there, axis=1, keepdims=True))
        here, there = jnp.exp(here - top), jnp.exp(there - top)
        inv = 1.0 / (jnp.sum(here, axis=1, keepdims=True) + jnp.sum(there, axis=1, keepdims=True))
        result = dot((here * inv).astype(BF), qkv[c, :, 4 * HK :]) + dot((there * inv).astype(BF), qkv[1 - c, :, 4 * HK :])
        attended = jnp.where(wide_lane < HV, result[:half], result[half:]).astype(BF)
        total = (pool[y, rows_here, :].astype(F32) + attended.astype(F32)).astype(BF)
        mixed[pl.ds(side * (ny // 2), ny // 2)] = total.reshape(ny // 2, half_rows, cols)

    mine_side = lax.div(y, ny // 2)
    far = (1 - mine_side) * (ny // 2)
    attend(1 - mine_side, True)
    for k in range(ny // 2):
        send(mixed.at[far + k], landed.at[y], r_mix.at[y], at(h, z, x, far + k, c))
    attend(mine_side, False)
    near = mine_side * (ny // 2) + lax.rem(y + 1, 2)
    send(mixed.at[near], landed.at[y], r_mix.at[y], at(h, z, x, near, c))
    landed[y] = mixed[y]
    for yy in others_y:
        arrived(landed.at[yy], r_mix.at[yy])
    for yy in range(ny):
        out_ref[:, yy * cols : (yy + 1) * cols] = landed[yy]

    for cp, when in pending:
        if when is None:
            cp.wait_send()
        else:
            pl.when(when)(cp.wait_send)


def shards(features, conv_weight, conv_bias, norm_gain, qkv_weight):
    dp, ny = lax.axis_size("dp"), lax.axis_size("seq") // 2
    nx, nz = NX, dp // (NH * NX)
    taps, rows, cols = conv_weight.shape
    cols, cin, width = 2 * cols, rows * dp, 2 * ny * cols
    half_rows = features.shape[1] // 2
    step, heads = qkv_weight.shape
    heads = 2 * heads
    positions = half_rows * ny
    dma = pltpu.SemaphoreType.DMA
    vmem = pltpu.VMEM
    ups, downs = nz // 2, nz - 1 - nz // 2
    count = len(PARTS)
    strips = pl.cdiv(2 * 2 * cin // 128, 16) * 16
    packed, p_packed = pl.cdiv(taps * rows, 16) * 16, pl.cdiv(step, 16) * 16
    sends = 4 + (ny - 1) + 1 + ny + 2 * (nx - 1) + count * (3 * nz - 2) + 2 * ny + (2 * nz - 1) + 1 + (ny - 1)
    scratch = [
        vmem(features.shape[1:], BF),
        vmem(conv_weight.shape, BF),
        vmem((width // 128, 128), F32),
        vmem((width // 128, 128), F32),
        vmem(qkv_weight.shape, BF),
        vmem((half_rows, 2 * cin), BF),
        vmem((ny, half_rows, 2 * cin), BF),
        vmem((strips, 128), BF),
        vmem((ny + 2, strips, 128), BF),
        vmem((cin // 128, 2 * half_rows, 128), F32),
        vmem((half_rows + 16, 2 * cin), F32),
        vmem((ny, half_rows, 2 * cin), BF),
        vmem((ny, half_rows, 2 * cin), BF),
        vmem((packed, 256), F32),
        vmem((packed, 256), BF),
        vmem((2, packed, 256), BF),
        vmem((nx, packed, cols), BF),
        vmem((packed, cols), F32),
        vmem((taps, nx * rows, cols), F32),
        vmem((2 * nz, taps, nx * rows, cols), BF),
        vmem((p_packed, 384), BF),
        vmem((2, p_packed, 384), BF),
        vmem((nx, p_packed, heads), BF),
        vmem((nx * step, heads), F32),
        vmem((width, heads), BF),
        vmem((ny, positions, cols), BF),
        vmem((2, positions, heads), BF),
        vmem((ny, half_rows, cols), BF),
        vmem((ny, half_rows, cols), BF),
        dma((5,)), dma((sends,)), dma((ny,)), dma((ny,)), dma((2,)), dma((2,)), dma((nx,)), dma((nx,)),
        dma((count, ups)), dma((count, max(downs, 1))),
        dma((count, nz)), dma((ups,)), dma((max(downs, 1),)), dma((nz,)),
        dma((ny // 2, ny)), dma((2,)), dma((ny,)),
    ]
    out = pl.pallas_call(
        functools.partial(kernel, nz, nx, ny),
        out_shape=jax.ShapeDtypeStruct((half_rows, width), BF),
        in_specs=[pl.BlockSpec(memory_space=pltpu.HBM)] * 5,
        out_specs=pl.BlockSpec(memory_space=pltpu.VMEM),
        scratch_shapes=scratch,
        compiler_params=pltpu.CompilerParams(
            collective_id=0, has_side_effects=True, vmem_limit_bytes=64 * 2**20
        ),
        name="section",
    )(
        features[0],
        conv_weight,
        conv_bias.reshape(width // 128, 128),
        norm_gain.reshape(width // 128, 128),
        qkv_weight,
    )
    return out[None]


def solution(mesh):
    return jax.shard_map(
        shards,
        mesh=mesh,
        in_specs=(P("dp", "seq", None), P(None, "dp", "seq"), P(), P(), P("dp", "seq")),
        out_specs=P("dp", "seq", None),
        check_vma=False,
    )
```

```python
import functools

import jax
import jax.numpy as jnp
from jax import lax
from jax.experimental import pallas as pl
from jax.experimental.pallas import tpu as pltpu
from jax.sharding import PartitionSpec as P

HK = 64
HV = 192
NH = 2
NX = 4
BF = jnp.bfloat16
F32 = jnp.float32
LAG = 3
GROUP = 128
STAGGER = 0


def kernel(
    nz, nx, ny,
    feat_in, conv_in, bias_in, gain_in, proj_in, out_ref,
    feat_ref, conv_ref, bias_ref, gain_ref, proj_ref,
    mine, feat, edge, edges, ext, wide, prev, later,
    wpack, wown, w0, w1, wflat32, wbuild, wc, pown, p0, p1, pbuild, pw,
    pool, qkv, mixed, landed,
    in_sems, send_sems, r_feat, r_edge, r_w0, r_p0, r_w1, r_p1,
    r_wa, r_wb, r_wsib, r_pool, r_kv, r_mix,
):
    dp, seq = lax.axis_index("dp"), lax.axis_index("seq")
    h, z, x = lax.div(dp, nz * nx), lax.rem(lax.div(dp, nx), nz), lax.rem(dp, nx)
    y, c = lax.div(seq, 2), lax.rem(seq, 2)
    turn = 1 - 2 * c

    def at(hh, zz, xx, yy, cc):
        return ((hh * nz + zz) * nx + xx, yy * 2 + cc)

    def round_z(offset):
        return lax.rem(z + offset + 2 * nz, nz)

    def round_x(offset):
        return lax.rem(x + offset + nx, nx)

    sibling = at(h, z, x, y, 1 - c)
    z_next, z_last = at(h, round_z(turn), x, y, c), at(h, round_z(-turn), x, y, c)
    x_next, x_last = at(h, z, round_x(turn), y, c), at(h, z, round_x(-turn), y, c)
    others_y = [lax.rem(y + d, ny) for d in (2, 1, 3)]
    others_x = [lax.rem(x + d, nx) for d in range(1, nx)]

    partners = [sibling, z_next, z_last, at(1 - h, z, x, y, 0), at(1 - h, z, x, y, 1)]
    partners += [at(h, z, x, yy, c) for yy in others_y]
    partners += [at(h, z, x, yy, 1 - c) for yy in others_y]
    partners += [at(h, z, xx, y, c) for xx in others_x]
    inputs = ((conv_in, conv_ref), (feat_in, feat_ref), (proj_in, proj_ref), (bias_in, bias_ref), (gain_in, gain_ref))
    loads = [pltpu.make_async_copy(src, dst, in_sems.at[i]) for i, (src, dst) in enumerate(inputs)]
    for load in loads:
        load.start()
    barrier = pltpu.get_barrier_semaphore()
    for device in partners:
        pl.semaphore_signal(barrier, inc=1, device_id=device, device_id_type=pl.DeviceIdType.MESH)

    for load in loads:
        load.wait()

    half_rows, lanes = mine.shape
    cin = lanes // 2
    for k in range(cin // 128):
        ext[k] = feat_ref[:, 128 * k : 128 * (k + 1)].astype(F32)
        mine[:, 128 * k : 128 * (k + 1)] = ext[k, pl.ds(0, half_rows, stride=2), :].astype(BF)
        mine[:, cin + 128 * k : cin + 128 * (k + 1)] = ext[k, pl.ds(1, half_rows, stride=2), :].astype(BF)
    first = mine[0:16, :].astype(F32)[0:1]
    last = mine[half_rows - 16 :, :].astype(F32)[15:16]
    strips = [row[:, 128 * k : 128 * (k + 1)] for row in (first, last) for k in range(lanes // 128)]
    spare = edge.shape[0] - len(strips)
    edge[...] = jnp.concatenate(strips + [jnp.zeros((spare, 128), F32)], axis=0).astype(BF)
    zero = jnp.zeros(edge.shape, BF)
    edges[0] = zero
    edges[ny + 1] = zero
    own = c == h
    taps, rows, cols = conv_ref.shape
    p_in, p_cols = proj_ref.shape
    wpack[...] = jnp.zeros(wpack.shape, F32)
    for t in range(taps):
        wpack[rows * t : rows * (t + 1), :cols] = conv_ref[t].astype(F32)
    wown[...] = wpack[...].astype(BF)
    pown[...] = jnp.zeros(pown.shape, BF)
    pown[:p_in, :p_cols] = proj_ref[...]

    @pl.when(own)
    def _():
        w0[c] = wown[...]
        p0[c] = pown[...]

    pl.semaphore_wait(barrier, len(partners))

    pending = []

    def copy(src, dst, recv, device, index):
        return pltpu.make_async_remote_copy(
            src_ref=src, dst_ref=dst, send_sem=send_sems.at[index], recv_sem=recv,
            device_id=device, device_id_type=pl.DeviceIdType.MESH,
        )

    def send(src, dst, recv, device, when=None):
        cp = copy(src, dst, recv, device, len(pending))
        if when is None:
            cp.start()
        else:
            pl.when(when)(cp.start)
        pending.append((cp, when))

    def arrived(dst, recv):
        copy(dst, dst, recv, sibling, 0).wait_recv()

    middle = jnp.logical_or(y == 1, y == 2)
    pass_from, pass_to = jnp.where(y == 1, 3, 0), jnp.where(y == 1, 0, 3)

    def spread(ref, dst, recv):
        for yy in others_y:
            send(ref, dst, recv.at[y], at(h, z, x, yy, c), jnp.abs(yy - y) < 3)

    def pass_on(block, recv):
        @pl.when(middle)
        def _():
            arrived(block(pass_from), recv.at[pass_from])

        send(block(pass_from), block(pass_from), recv.at[pass_from], at(h, z, x, pass_to, c), middle)

    def rest(block, recv):
        for yy in others_y:
            @pl.when(jnp.logical_not(jnp.logical_and(middle, yy == pass_from)))
            def _():
                arrived(block(yy), recv.at[yy])

    other = jnp.logical_not(own)
    send(wown, w0.at[c], r_w0.at[c], at(1 - h, z, x, y, h))
    send(wown, w0.at[c], r_w0.at[c], sibling, other)

    feat[y] = mine[...]
    spread(mine, feat.at[y], r_feat)
    for yy in others_y:
        send(edge, edges.at[1 + y], r_edge.at[y], at(h, z, x, yy, 1 - c))
    send(edge, edges.at[1 + y], r_edge.at[y], sibling)
    send(pown, p0.at[c], r_p0.at[c], at(1 - h, z, x, y, h))
    send(pown, p0.at[c], r_p0.at[c], sibling, other)

    arrived(w0.at[1 - c], r_w0.at[1 - c])

    @pl.when(other)
    def _():
        arrived(w0.at[c], r_w0.at[c])

    w1[x] = jnp.concatenate([w0[0].astype(F32)[:, :cols], w0[1].astype(F32)[:, :cols]], axis=1).astype(BF)
    for xx in others_x:
        send(w1.at[x], w1.at[x], r_w1.at[x], at(h, z, xx, y, c))

    w_rows = rows * nx
    p_rows = p_in * nx
    ups, downs = nz // 2, nz - 1 - nz // 2
    count = wc.shape[0]

    def carried(distance):
        return lax.rem(z + x + c + distance, 2) == 0

    for xx in others_x:
        arrived(w1.at[xx], r_w1.at[xx])
    for xx in range(nx):
        wflat32[...] = w1[xx].astype(F32)
        for t in range(taps):
            wbuild[t, rows * xx : rows * (xx + 1), :] = wflat32[rows * t : rows * (t + 1), :]
    for j in range(count):
        wc[j, c * nz + z] = wbuild[:, :, GROUP * j : GROUP * (j + 1)].astype(BF)

    def w_block(j, cc, zz):
        if j == count:
            return pw.at[pl.ds(pl.multiple_of((cc * nz + zz) * p_rows, 16), p_rows), :]
        return wc.at[j, cc * nz + zz]

    to_sibling = {}

    def w_start(j):
        block = w_block(j, c, z)
        send(block, block, r_wa.at[j, 0], z_next, carried(0))
        if downs:
            send(block, block, r_wb.at[j, 0], z_last, carried(0))
        send(block, block, r_wsib.at[j, 0], sibling)

    def ways(d):
        found = [(round_z(-turn * (1 + d)), r_wa, ups, z_next, x_next, 1 + d)]
        if d < downs:
            found.append((round_z(turn * (1 + d)), r_wb, downs, z_last, x_last, 1 + ups + d))
        return found

    def w_step(j, d):
        for zz, recv, steps, z_to, x_to, k in ways(d):
            block = w_block(j, c, zz)

            @pl.when(carried(1 + d))
            def _():
                arrived(block, recv.at[j, d])

            if d + 1 < steps:
                send(block, block, recv.at[j, d + 1], z_to, carried(1 + d))
        for zz, recv, steps, z_to, x_to, k in ways(d):
            block = w_block(j, c, zz)
            send(block, block, recv.at[j, d], x_to, carried(1 + d))
            cp = copy(block, block, r_wsib.at[j, k], sibling, len(pending))
            pl.when(carried(1 + d))(cp.start)
            pending.append((cp, None))
            to_sibling[j, k] = cp

    def w_finish(j, d):
        for zz, recv, steps, z_to, x_to, k in ways(d):
            @pl.when(carried(d))
            def _():
                arrived(w_block(j, c, zz), recv.at[j, d])
                to_sibling[j, k].start()

    def w_sibling(j):
        zs = [z] + [round_z(turn * (1 + d)) for d in range(ups)] + [round_z(-turn * (1 + d)) for d in range(downs)]
        for k, zz in enumerate(zs):
            arrived(w_block(j, 1 - c, zz), r_wsib.at[j, k])

    def p_join():
        arrived(p0.at[1 - c], r_p0.at[1 - c])

        @pl.when(other)
        def _():
            arrived(p0.at[c], r_p0.at[c])

        a, b = p0[0].astype(F32)[:, :p_cols], p0[1].astype(F32)[:, :p_cols]
        p1[x] = jnp.concatenate(
            [a[:, :HK], b[:, :HK], a[:, HK : 2 * HK], b[:, HK : 2 * HK], a[:, 2 * HK :], b[:, 2 * HK :]],
            axis=1,
        ).astype(BF)
        for xx in others_x:
            send(p1.at[x], p1.at[x], r_p1.at[x], at(h, z, xx, y, c))

    def p_start():
        for xx in others_x:
            arrived(p1.at[xx], r_p1.at[xx])
        for xx in range(nx):
            pbuild[p_in * xx : p_in * (xx + 1), :] = p1[xx].astype(F32)[:p_in]
        pw[pl.ds(pl.multiple_of((c * nz + z) * p_rows, 16), p_rows), :] = pbuild[...].astype(BF)
        w_start(count)

    def p_slot(k):
        if k == 0:
            p_start()
        if 0 < k <= ups:
            w_step(count, k - 1)
        if 1 < k <= ups + 1:
            w_finish(count, k - 2)

    def conv_inputs():
        for yy in others_y:
            arrived(edges.at[1 + yy], r_edge.at[yy])
        arrived(edges.at[1 + y], r_edge.at[y])
        rest(lambda yy: feat.at[yy], r_feat)
        for yy in range(ny):
            wide[8 : 8 + half_rows, :] = feat[yy].astype(F32)
            before, after = edges[yy + c].astype(F32), edges[yy + c + 1].astype(F32)
            for k in range(lanes // 128):
                wide[7:8, 128 * k : 128 * (k + 1)] = before[lanes // 128 + k : lanes // 128 + k + 1]
                wide[8 + half_rows : 9 + half_rows, 128 * k : 128 * (k + 1)] = after[k : k + 1]
            prev[yy] = wide[7 : 7 + half_rows, :].astype(BF)
            later[yy] = wide[9 : 9 + half_rows, :].astype(BF)

    for t in range(ups + 2 + STAGGER * (count - 1)):
        for j in range(count):
            k = t - STAGGER * j
            if k == 0:
                w_start(j)
            if 0 < k <= ups:
                w_step(j, k - 1)
            if 1 < k <= ups + 1:
                w_finish(j, k - 2)
        if t == 0:
            p_join()
        if t == 1:
            pass_on(lambda yy: feat.at[yy], r_feat)
        if t >= LAG and t - LAG < ups + 2:
            p_slot(t - LAG)
        if t == ups - 1:
            conv_inputs()

    cols = count * GROUP

    def dot(left, right):
        return jnp.dot(left, right, preferred_element_type=F32)

    def gelu(value, bias):
        value = value + bias
        inner = 0.7978845608028654 * (value + 0.044715 * (value * value * value))
        return value * (0.5 * (1.0 + jnp.tanh(inner)))

    def pool_part(j):
        return lambda yy: pool.at[yy, j]

    def whole(yy, rows_here=slice(None)):
        return jnp.concatenate([pool[yy, j, rows_here, :].astype(F32) for j in range(count)], axis=1)

    def conv(j):
        bias = bias_ref[pl.ds(y * (cols // 128) + j, 1), :]

        def flat(ref):
            return ref[...].reshape(ny * half_rows, lanes)

        before, now, after = flat(prev), flat(feat), flat(later)
        taken = [before[:, :cin], before[:, cin:], now[:, :cin], now[:, cin:], after[:, :cin], after[:, cin:]]
        total = None
        for t in range(taps):
            part_sum = dot(jnp.concatenate([taken[t], taken[t + 1]], axis=0), wc[j, :, t].reshape(cin, GROUP))
            total = part_sum if total is None else total + part_sum
        even, odd = total[: ny * half_rows], total[ny * half_rows :]
        pool[y, j] = jnp.maximum(gelu(even, bias), gelu(odd, bias)).astype(BF)

    left = list(range(max(ups + 2 + STAGGER * (count - 1) - LAG, 0), ups + 2))
    for j in range(count):
        w_sibling(j)
        conv(j)
        spread(pool_part(j)(y), pool_part(j)(y), r_pool.at[j])
        if left and j:
            p_slot(left.pop(0))
    for j in range(count):
        pass_on(pool_part(j), r_pool.at[j])
        if left:
            p_slot(left.pop(0))
    for k in left:
        p_slot(k)
    w_sibling(count)

    for j in range(count):
        rest(pool_part(j), r_pool.at[j])
    width = ny * cols
    total = functools.reduce(
        jnp.add, [jnp.sum(whole(yy), axis=1, keepdims=True) for yy in range(ny)]
    )
    mean = total * (1.0 / width)
    square = functools.reduce(
        jnp.add, [jnp.sum(jnp.square(whole(yy) - mean), axis=1, keepdims=True) for yy in range(ny)]
    )
    inverse = 1.0 / jnp.sqrt(square * (1.0 / width) + 1e-05)

    def gain(yy):
        k = cols // 128
        return jnp.concatenate([gain_ref[yy * k + i : yy * k + i + 1, :] for i in range(k)], axis=1)

    acc = None
    for yy in range(ny):
        normed = ((whole(yy) - mean) * inverse * gain(yy)).astype(BF)
        part = dot(normed, pw[yy * cols : (yy + 1) * cols, :])
        acc = part if acc is None else acc + part
    qkv[c] = acc.astype(BF)
    send(qkv.at[c], qkv.at[c], r_kv.at[c], sibling)

    half = half_rows * ny // 2
    lane = lax.broadcasted_iota(jnp.int32, (half, 2 * HK), 1)
    wide_lane = lax.broadcasted_iota(jnp.int32, (half, cols), 1)

    def attend(side, first):
        rows_here = pl.ds(pl.multiple_of(side * half, half), half)
        query = qkv[c, rows_here, : 2 * HK]
        none = jnp.zeros_like(query)
        both = jnp.concatenate([jnp.where(lane < HK, query, none), jnp.where(lane < HK, none, query)], axis=0)

        def score(core):
            keys = qkv[core, :, 2 * HK : 4 * HK]
            return lax.dot_general(both, keys, (((1,), (1,)), ((), ())), preferred_element_type=F32) * (HK ** -0.5)

        here = score(c)
        if first:
            arrived(qkv.at[1 - c], r_kv.at[1 - c])
        there = score(1 - c)
        top = jnp.maximum(jnp.max(here, axis=1, keepdims=True), jnp.max(there, axis=1, keepdims=True))
        here, there = jnp.exp(here - top), jnp.exp(there - top)
        inv = 1.0 / (jnp.sum(here, axis=1, keepdims=True) + jnp.sum(there, axis=1, keepdims=True))
        result = dot((here * inv).astype(BF), qkv[c, :, 4 * HK :]) + dot((there * inv).astype(BF), qkv[1 - c, :, 4 * HK :])
        attended = jnp.where(wide_lane < HV, result[:half], result[half:]).astype(BF)
        total = (whole(y, rows_here) + attended.astype(F32)).astype(BF)
        mixed[pl.ds(side * (ny // 2), ny // 2)] = total.reshape(ny // 2, half_rows, cols)

    mine_side = lax.div(y, ny // 2)
    far = (1 - mine_side) * (ny // 2)
    attend(1 - mine_side, True)
    for k in range(ny // 2):
        send(mixed.at[far + k], landed.at[y], r_mix.at[y], at(h, z, x, far + k, c))
    attend(mine_side, False)
    near = mine_side * (ny // 2) + lax.rem(y + 1, 2)
    send(mixed.at[near], landed.at[y], r_mix.at[y], at(h, z, x, near, c))
    landed[y] = mixed[y]
    writes = []
    for i, yy in enumerate([y] + others_y):
        if i:
            arrived(landed.at[yy], r_mix.at[yy])
        column = pl.multiple_of(yy * cols, 128)
        writes.append(pltpu.make_async_copy(landed.at[yy], out_ref.at[:, pl.ds(column, cols)], in_sems.at[i]))
        writes[-1].start()
    for write in writes:
        write.wait()

    for cp, when in pending:
        if when is None:
            cp.wait_send()
        else:
            pl.when(when)(cp.wait_send)


def shards(features, conv_weight, conv_bias, norm_gain, qkv_weight):
    dp, ny = lax.axis_size("dp"), lax.axis_size("seq") // 2
    nx, nz = NX, dp // (NH * NX)
    taps, rows, cols = conv_weight.shape
    cols, cin, width = 2 * cols, rows * dp, 2 * ny * cols
    half_rows = features.shape[1] // 2
    step, heads = qkv_weight.shape
    heads = 2 * heads
    positions = half_rows * ny
    dma = pltpu.SemaphoreType.DMA
    vmem = pltpu.VMEM
    ups, downs = nz // 2, nz - 1 - nz // 2
    count = cols // GROUP
    strips = pl.cdiv(2 * 2 * cin // 128, 16) * 16
    packed, p_packed = pl.cdiv(taps * rows, 16) * 16, pl.cdiv(step, 16) * 16
    sends = 4 + (ny - 1) + 1 + ny + 2 * (nx - 1) + (count + 1) * (3 * nz - 2) + count * ny + 1 + (ny - 1)
    scratch = [
        vmem(features.shape[1:], BF),
        vmem(conv_weight.shape, BF),
        vmem((width // 128, 128), F32),
        vmem((width // 128, 128), F32),
        vmem(qkv_weight.shape, BF),
        vmem((half_rows, 2 * cin), BF),
        vmem((ny, half_rows, 2 * cin), BF),
        vmem((strips, 128), BF),
        vmem((ny + 2, strips, 128), BF),
        vmem((cin // 128, 2 * half_rows, 128), F32),
        vmem((half_rows + 16, 2 * cin), F32),
        vmem((ny, half_rows, 2 * cin), BF),
        vmem((ny, half_rows, 2 * cin), BF),
        vmem((packed, 256), F32),
        vmem((packed, 256), BF),
        vmem((2, packed, 256), BF),
        vmem((nx, packed, cols), BF),
        vmem((packed, cols), F32),
        vmem((taps, nx * rows, cols), F32),
        vmem((count, 2 * nz, taps, nx * rows, GROUP), BF),
        vmem((p_packed, 384), BF),
        vmem((2, p_packed, 384), BF),
        vmem((nx, p_packed, heads), BF),
        vmem((nx * step, heads), F32),
        vmem((width, heads), BF),
        vmem((ny, count, positions, GROUP), BF),
        vmem((2, positions, heads), BF),
        vmem((ny, half_rows, cols), BF),
        vmem((ny, half_rows, cols), BF),
        dma((5,)), dma((sends,)), dma((ny,)), dma((ny,)), dma((2,)), dma((2,)), dma((nx,)), dma((nx,)),
        dma((count + 1, ups)), dma((count + 1, max(downs, 1))), dma((count + 1, nz)),
        dma((count, ny)), dma((2,)), dma((ny,)),
    ]
    out = pl.pallas_call(
        functools.partial(kernel, nz, nx, ny),
        out_shape=jax.ShapeDtypeStruct((half_rows, width), BF),
        in_specs=[pl.BlockSpec(memory_space=pltpu.HBM)] * 5,
        out_specs=pl.BlockSpec(memory_space=pltpu.HBM),
        scratch_shapes=scratch,
        compiler_params=pltpu.CompilerParams(
            collective_id=0, has_side_effects=True, vmem_limit_bytes=64 * 2**20
        ),
        name="section",
    )(
        features[0],
        conv_weight,
        conv_bias.reshape(width // 128, 128),
        norm_gain.reshape(width // 128, 128),
        qkv_weight,
    )
    return out[None]


def solution(mesh):
    return jax.shard_map(
        shards,
        mesh=mesh,
        in_specs=(P("dp", "seq", None), P(None, "dp", "seq"), P(), P(), P("dp", "seq")),
        out_specs=P("dp", "seq", None),
        check_vma=False,
    )
```

```python
import functools

import jax
import jax.numpy as jnp
from jax import lax
from jax.experimental import pallas as pl
from jax.experimental.pallas import tpu as pltpu
from jax.sharding import PartitionSpec as P

HK = 64
HV = 192
NH = 2
NX = 4
BF = jnp.bfloat16
F32 = jnp.float32
LAG = 3
GROUP = 128
STAGGER = 0


def kernel(
    nz, nx, ny,
    feat_in, conv_in, bias_in, gain_in, proj_in, out_ref,
    feat_ref, conv_ref, bias_ref, gain_ref, proj_ref,
    mine, feat, edge, edges, ext, wide, prev, later,
    wpack, wown, w0, w1, wflat32, wbuild, wc, pown, p0, p1, pbuild, pw,
    pool, qkv, mixed, landed,
    in_sems, send_sems, r_feat, r_edge, r_w0, r_p0, r_w1, r_p1,
    r_wa, r_wb, r_wsib, r_pool, r_kv, r_mix,
):
    dp, seq = lax.axis_index("dp"), lax.axis_index("seq")
    h, z, x = lax.div(dp, nz * nx), lax.rem(lax.div(dp, nx), nz), lax.rem(dp, nx)
    y, c = lax.div(seq, 2), lax.rem(seq, 2)
    turn = 1 - 2 * c

    def at(hh, zz, xx, yy, cc):
        return ((hh * nz + zz) * nx + xx, yy * 2 + cc)

    def round_z(offset):
        return lax.rem(z + offset + 2 * nz, nz)

    def round_x(offset):
        return lax.rem(x + offset + nx, nx)

    sibling = at(h, z, x, y, 1 - c)
    z_next, z_last = at(h, round_z(turn), x, y, c), at(h, round_z(-turn), x, y, c)
    x_next, x_last = at(h, z, round_x(turn), y, c), at(h, z, round_x(-turn), y, c)
    others_y = [lax.rem(y + d, ny) for d in (2, 1, 3)]
    others_x = [lax.rem(x + d, nx) for d in range(1, nx)]

    partners = [sibling, z_next, z_last, at(1 - h, z, x, y, 0), at(1 - h, z, x, y, 1)]
    partners += [at(h, z, x, yy, c) for yy in others_y]
    partners += [at(h, z, x, yy, 1 - c) for yy in others_y]
    partners += [at(h, z, xx, y, c) for xx in others_x]
    inputs = ((conv_in, conv_ref), (feat_in, feat_ref), (proj_in, proj_ref), (bias_in, bias_ref), (gain_in, gain_ref))
    loads = [pltpu.make_async_copy(src, dst, in_sems.at[i]) for i, (src, dst) in enumerate(inputs)]
    for load in loads:
        load.start()
    barrier = pltpu.get_barrier_semaphore()
    for device in partners:
        pl.semaphore_signal(barrier, inc=1, device_id=device, device_id_type=pl.DeviceIdType.MESH)

    for load in loads:
        load.wait()

    half_rows, lanes = mine.shape
    cin = lanes // 2
    for k in range(cin // 128):
        ext[k] = feat_ref[:, 128 * k : 128 * (k + 1)].astype(F32)
        mine[:, 128 * k : 128 * (k + 1)] = ext[k, pl.ds(0, half_rows, stride=2), :].astype(BF)
        mine[:, cin + 128 * k : cin + 128 * (k + 1)] = ext[k, pl.ds(1, half_rows, stride=2), :].astype(BF)
    first = mine[0:16, :].astype(F32)[0:1]
    last = mine[half_rows - 16 :, :].astype(F32)[15:16]
    strips = [row[:, 128 * k : 128 * (k + 1)] for row in (first, last) for k in range(lanes // 128)]
    spare = edge.shape[0] - len(strips)
    edge[...] = jnp.concatenate(strips + [jnp.zeros((spare, 128), F32)], axis=0).astype(BF)
    zero = jnp.zeros(edge.shape, BF)
    edges[0] = zero
    edges[ny + 1] = zero
    own = c == h
    taps, rows, cols = conv_ref.shape
    p_in, p_cols = proj_ref.shape
    wpack[...] = jnp.zeros(wpack.shape, F32)
    for t in range(taps):
        wpack[rows * t : rows * (t + 1), :cols] = conv_ref[t].astype(F32)
    wown[...] = wpack[...].astype(BF)
    pown[...] = jnp.zeros(pown.shape, BF)
    pown[:p_in, :p_cols] = proj_ref[...]

    @pl.when(own)
    def _():
        w0[c] = wown[...]
        p0[c] = pown[...]

    pl.semaphore_wait(barrier, len(partners))

    pending = []

    def copy(src, dst, recv, device, index):
        return pltpu.make_async_remote_copy(
            src_ref=src, dst_ref=dst, send_sem=send_sems.at[index], recv_sem=recv,
            device_id=device, device_id_type=pl.DeviceIdType.MESH,
        )

    def send(src, dst, recv, device, when=None):
        cp = copy(src, dst, recv, device, len(pending))
        if when is None:
            cp.start()
        else:
            pl.when(when)(cp.start)
        pending.append((cp, when))

    def arrived(dst, recv):
        copy(dst, dst, recv, sibling, 0).wait_recv()

    middle = jnp.logical_or(y == 1, y == 2)
    pass_from, pass_to = jnp.where(y == 1, 3, 0), jnp.where(y == 1, 0, 3)

    def spread(ref, dst, recv):
        for yy in others_y:
            send(ref, dst, recv.at[y], at(h, z, x, yy, c), jnp.abs(yy - y) < 3)

    def pass_on(block, recv):
        @pl.when(middle)
        def _():
            arrived(block(pass_from), recv.at[pass_from])

        send(block(pass_from), block(pass_from), recv.at[pass_from], at(h, z, x, pass_to, c), middle)

    def rest(block, recv):
        for yy in others_y:
            @pl.when(jnp.logical_not(jnp.logical_and(middle, yy == pass_from)))
            def _():
                arrived(block(yy), recv.at[yy])

    other = jnp.logical_not(own)
    send(wown, w0.at[c], r_w0.at[c], at(1 - h, z, x, y, h))
    send(wown, w0.at[c], r_w0.at[c], sibling, other)

    feat[y] = mine[...]
    spread(mine, feat.at[y], r_feat)
    for yy in others_y:
        send(edge, edges.at[1 + y], r_edge.at[y], at(h, z, x, yy, 1 - c))
    send(edge, edges.at[1 + y], r_edge.at[y], sibling)
    send(pown, p0.at[c], r_p0.at[c], at(1 - h, z, x, y, h))
    send(pown, p0.at[c], r_p0.at[c], sibling, other)

    arrived(w0.at[1 - c], r_w0.at[1 - c])

    @pl.when(other)
    def _():
        arrived(w0.at[c], r_w0.at[c])

    w1[x] = jnp.concatenate([w0[0].astype(F32)[:, :cols], w0[1].astype(F32)[:, :cols]], axis=1).astype(BF)
    for xx in others_x:
        send(w1.at[x], w1.at[x], r_w1.at[x], at(h, z, xx, y, c))

    w_rows = rows * nx
    p_rows = p_in * nx
    ups, downs = nz // 2, nz - 1 - nz // 2
    count = wc.shape[0]

    def carried(distance):
        return lax.rem(z + x + c + distance, 2) == 0

    for xx in others_x:
        arrived(w1.at[xx], r_w1.at[xx])
    for xx in range(nx):
        wflat32[...] = w1[xx].astype(F32)
        for t in range(taps):
            wbuild[t, rows * xx : rows * (xx + 1), :] = wflat32[rows * t : rows * (t + 1), :]
    for j in range(count):
        wc[j, c * nz + z] = wbuild[:, :, GROUP * j : GROUP * (j + 1)].astype(BF)

    def w_block(j, cc, zz):
        if j == count:
            return pw.at[pl.ds(pl.multiple_of((cc * nz + zz) * p_rows, 16), p_rows), :]
        return wc.at[j, cc * nz + zz]

    to_sibling = {}

    def w_start(j):
        block = w_block(j, c, z)
        send(block, block, r_wa.at[j, 0], z_next, carried(0))
        if downs:
            send(block, block, r_wb.at[j, 0], z_last, carried(0))
        send(block, block, r_wsib.at[j, 0], sibling)

    def ways(d):
        found = [(round_z(-turn * (1 + d)), r_wa, ups, z_next, x_next, 1 + d)]
        if d < downs:
            found.append((round_z(turn * (1 + d)), r_wb, downs, z_last, x_last, 1 + ups + d))
        return found

    def w_step(j, d):
        for zz, recv, steps, z_to, x_to, k in ways(d):
            block = w_block(j, c, zz)

            @pl.when(carried(1 + d))
            def _():
                arrived(block, recv.at[j, d])

            if d + 1 < steps:
                send(block, block, recv.at[j, d + 1], z_to, carried(1 + d))
        for zz, recv, steps, z_to, x_to, k in ways(d):
            block = w_block(j, c, zz)
            send(block, block, recv.at[j, d], x_to, carried(1 + d))
            cp = copy(block, block, r_wsib.at[j, k], sibling, len(pending))
            pl.when(carried(1 + d))(cp.start)
            pending.append((cp, None))
            to_sibling[j, k] = cp

    def w_finish(j, d):
        for zz, recv, steps, z_to, x_to, k in ways(d):
            @pl.when(carried(d))
            def _():
                arrived(w_block(j, c, zz), recv.at[j, d])
                to_sibling[j, k].start()

    def w_sibling(j):
        zs = [z] + [round_z(turn * (1 + d)) for d in range(ups)] + [round_z(-turn * (1 + d)) for d in range(downs)]
        for k, zz in enumerate(zs):
            arrived(w_block(j, 1 - c, zz), r_wsib.at[j, k])

    def p_join():
        arrived(p0.at[1 - c], r_p0.at[1 - c])

        @pl.when(other)
        def _():
            arrived(p0.at[c], r_p0.at[c])

        a, b = p0[0].astype(F32)[:, :p_cols], p0[1].astype(F32)[:, :p_cols]
        p1[x] = jnp.concatenate(
            [a[:, :HK], b[:, :HK], a[:, HK : 2 * HK], b[:, HK : 2 * HK], a[:, 2 * HK :], b[:, 2 * HK :]],
            axis=1,
        ).astype(BF)
        for xx in others_x:
            send(p1.at[x], p1.at[x], r_p1.at[x], at(h, z, xx, y, c))

    def p_start():
        for xx in others_x:
            arrived(p1.at[xx], r_p1.at[xx])
        for xx in range(nx):
            pbuild[p_in * xx : p_in * (xx + 1), :] = p1[xx].astype(F32)[:p_in]
        pw[pl.ds(pl.multiple_of((c * nz + z) * p_rows, 16), p_rows), :] = pbuild[...].astype(BF)
        w_start(count)

    def p_slot(k):
        if k == 0:
            p_start()
        if 0 < k <= ups:
            w_step(count, k - 1)
        if 1 < k <= ups + 1:
            w_finish(count, k - 2)

    def conv_inputs():
        for yy in others_y:
            arrived(edges.at[1 + yy], r_edge.at[yy])
        arrived(edges.at[1 + y], r_edge.at[y])
        rest(lambda yy: feat.at[yy], r_feat)
        for yy in range(ny):
            wide[8 : 8 + half_rows, :] = feat[yy].astype(F32)
            before, after = edges[yy + c].astype(F32), edges[yy + c + 1].astype(F32)
            for k in range(lanes // 128):
                wide[7:8, 128 * k : 128 * (k + 1)] = before[lanes // 128 + k : lanes // 128 + k + 1]
                wide[8 + half_rows : 9 + half_rows, 128 * k : 128 * (k + 1)] = after[k : k + 1]
            prev[yy] = wide[7 : 7 + half_rows, :].astype(BF)
            later[yy] = wide[9 : 9 + half_rows, :].astype(BF)

    for t in range(ups + 2 + STAGGER * (count - 1)):
        for j in range(count):
            k = t - STAGGER * j
            if k == 0:
                w_start(j)
            if 0 < k <= ups:
                w_step(j, k - 1)
            if 1 < k <= ups + 1:
                w_finish(j, k - 2)
        if t == 0:
            p_join()
        if t == 1:
            pass_on(lambda yy: feat.at[yy], r_feat)
        if t >= LAG and t - LAG < ups + 2:
            p_slot(t - LAG)
        if t == ups - 1:
            conv_inputs()

    cols = count * GROUP

    def dot(left, right):
        return jnp.dot(left, right, preferred_element_type=F32)

    def gelu(value, bias):
        value = value + bias
        inner = 0.7978845608028654 * (value + 0.044715 * (value * value * value))
        return value * (0.5 * (1.0 + jnp.tanh(inner)))

    def pool_part(j):
        return lambda yy: pool.at[yy, j]

    def whole(yy, rows_here=slice(None)):
        return jnp.concatenate([pool[yy, j, rows_here, :].astype(F32) for j in range(count)], axis=1)

    def conv(j):
        bias = bias_ref[pl.ds(y * (cols // 128) + j, 1), :]

        def flat(ref):
            return ref[...].reshape(ny * half_rows, lanes)

        before, now, after = flat(prev), flat(feat), flat(later)
        taken = [before[:, :cin], before[:, cin:], now[:, :cin], now[:, cin:], after[:, :cin], after[:, cin:]]
        total = None
        for t in range(taps):
            part_sum = dot(jnp.concatenate([taken[t], taken[t + 1]], axis=0), wc[j, :, t].reshape(cin, GROUP))
            total = part_sum if total is None else total + part_sum
        even, odd = total[: ny * half_rows], total[ny * half_rows :]
        pool[y, j] = jnp.maximum(gelu(even, bias), gelu(odd, bias)).astype(BF)

    left = list(range(max(ups + 2 + STAGGER * (count - 1) - LAG, 0), ups + 2))
    for j in range(count):
        w_sibling(j)
        conv(j)
        spread(pool_part(j)(y), pool_part(j)(y), r_pool.at[j])
        if left and j:
            p_slot(left.pop(0))
        if j:
            pass_on(pool_part(j - 1), r_pool.at[j - 1])
    pass_on(pool_part(count - 1), r_pool.at[count - 1])
    for k in left:
        p_slot(k)
    w_sibling(count)

    for j in range(count):
        rest(pool_part(j), r_pool.at[j])
    width = ny * cols
    total = functools.reduce(
        jnp.add, [jnp.sum(whole(yy), axis=1, keepdims=True) for yy in range(ny)]
    )
    mean = total * (1.0 / width)
    square = functools.reduce(
        jnp.add, [jnp.sum(jnp.square(whole(yy) - mean), axis=1, keepdims=True) for yy in range(ny)]
    )
    inverse = 1.0 / jnp.sqrt(square * (1.0 / width) + 1e-05)

    def gain(yy):
        k = cols // 128
        return jnp.concatenate([gain_ref[yy * k + i : yy * k + i + 1, :] for i in range(k)], axis=1)

    acc = None
    for yy in range(ny):
        normed = ((whole(yy) - mean) * inverse * gain(yy)).astype(BF)
        part = dot(normed, pw[yy * cols : (yy + 1) * cols, :])
        acc = part if acc is None else acc + part
    qkv[c] = acc.astype(BF)
    send(qkv.at[c], qkv.at[c], r_kv.at[c], sibling)

    half = half_rows * ny // 2
    lane = lax.broadcasted_iota(jnp.int32, (half, 2 * HK), 1)
    wide_lane = lax.broadcasted_iota(jnp.int32, (half, cols), 1)

    def attend(side, first):
        rows_here = pl.ds(pl.multiple_of(side * half, half), half)
        query = qkv[c, rows_here, : 2 * HK]
        none = jnp.zeros_like(query)
        both = jnp.concatenate([jnp.where(lane < HK, query, none), jnp.where(lane < HK, none, query)], axis=0)

        def score(core):
            keys = qkv[core, :, 2 * HK : 4 * HK]
            return lax.dot_general(both, keys, (((1,), (1,)), ((), ())), preferred_element_type=F32) * (HK ** -0.5)

        here = score(c)
        if first:
            arrived(qkv.at[1 - c], r_kv.at[1 - c])
        there = score(1 - c)
        top = jnp.maximum(jnp.max(here, axis=1, keepdims=True), jnp.max(there, axis=1, keepdims=True))
        here, there = jnp.exp(here - top), jnp.exp(there - top)
        inv = 1.0 / (jnp.sum(here, axis=1, keepdims=True) + jnp.sum(there, axis=1, keepdims=True))
        result = dot((here * inv).astype(BF), qkv[c, :, 4 * HK :]) + dot((there * inv).astype(BF), qkv[1 - c, :, 4 * HK :])
        attended = jnp.where(wide_lane < HV, result[:half], result[half:]).astype(BF)
        total = (whole(y, rows_here) + attended.astype(F32)).astype(BF)
        mixed[pl.ds(side * (ny // 2), ny // 2)] = total.reshape(ny // 2, half_rows, cols)

    mine_side = lax.div(y, ny // 2)
    far = (1 - mine_side) * (ny // 2)
    attend(1 - mine_side, True)
    for k in range(ny // 2):
        send(mixed.at[far + k], landed.at[y], r_mix.at[y], at(h, z, x, far + k, c))
    attend(mine_side, False)
    near = mine_side * (ny // 2) + lax.rem(y + 1, 2)
    send(mixed.at[near], landed.at[y], r_mix.at[y], at(h, z, x, near, c))
    landed[y] = mixed[y]
    writes = []
    for i, yy in enumerate([y] + others_y):
        if i:
            arrived(landed.at[yy], r_mix.at[yy])
        column = pl.multiple_of(yy * cols, 128)
        writes.append(pltpu.make_async_copy(landed.at[yy], out_ref.at[:, pl.ds(column, cols)], in_sems.at[i]))
        writes[-1].start()
    for write in writes:
        write.wait()

    for cp, when in pending:
        if when is None:
            cp.wait_send()
        else:
            pl.when(when)(cp.wait_send)


def shards(features, conv_weight, conv_bias, norm_gain, qkv_weight):
    dp, ny = lax.axis_size("dp"), lax.axis_size("seq") // 2
    nx, nz = NX, dp // (NH * NX)
    taps, rows, cols = conv_weight.shape
    cols, cin, width = 2 * cols, rows * dp, 2 * ny * cols
    half_rows = features.shape[1] // 2
    step, heads = qkv_weight.shape
    heads = 2 * heads
    positions = half_rows * ny
    dma = pltpu.SemaphoreType.DMA
    vmem = pltpu.VMEM
    ups, downs = nz // 2, nz - 1 - nz // 2
    count = cols // GROUP
    strips = pl.cdiv(2 * 2 * cin // 128, 16) * 16
    packed, p_packed = pl.cdiv(taps * rows, 16) * 16, pl.cdiv(step, 16) * 16
    sends = 4 + (ny - 1) + 1 + ny + 2 * (nx - 1) + (count + 1) * (3 * nz - 2) + count * ny + 1 + (ny - 1)
    scratch = [
        vmem(features.shape[1:], BF),
        vmem(conv_weight.shape, BF),
        vmem((width // 128, 128), F32),
        vmem((width // 128, 128), F32),
        vmem(qkv_weight.shape, BF),
        vmem((half_rows, 2 * cin), BF),
        vmem((ny, half_rows, 2 * cin), BF),
        vmem((strips, 128), BF),
        vmem((ny + 2, strips, 128), BF),
        vmem((cin // 128, 2 * half_rows, 128), F32),
        vmem((half_rows + 16, 2 * cin), F32),
        vmem((ny, half_rows, 2 * cin), BF),
        vmem((ny, half_rows, 2 * cin), BF),
        vmem((packed, 256), F32),
        vmem((packed, 256), BF),
        vmem((2, packed, 256), BF),
        vmem((nx, packed, cols), BF),
        vmem((packed, cols), F32),
        vmem((taps, nx * rows, cols), F32),
        vmem((count, 2 * nz, taps, nx * rows, GROUP), BF),
        vmem((p_packed, 384), BF),
        vmem((2, p_packed, 384), BF),
        vmem((nx, p_packed, heads), BF),
        vmem((nx * step, heads), F32),
        vmem((width, heads), BF),
        vmem((ny, count, positions, GROUP), BF),
        vmem((2, positions, heads), BF),
        vmem((ny, half_rows, cols), BF),
        vmem((ny, half_rows, cols), BF),
        dma((5,)), dma((sends,)), dma((ny,)), dma((ny,)), dma((2,)), dma((2,)), dma((nx,)), dma((nx,)),
        dma((count + 1, ups)), dma((count + 1, max(downs, 1))), dma((count + 1, nz)),
        dma((count, ny)), dma((2,)), dma((ny,)),
    ]
    out = pl.pallas_call(
        functools.partial(kernel, nz, nx, ny),
        out_shape=jax.ShapeDtypeStruct((half_rows, width), BF),
        in_specs=[pl.BlockSpec(memory_space=pltpu.HBM)] * 5,
        out_specs=pl.BlockSpec(memory_space=pltpu.HBM),
        scratch_shapes=scratch,
        compiler_params=pltpu.CompilerParams(
            collective_id=0, has_side_effects=True, vmem_limit_bytes=64 * 2**20
        ),
        name="section",
    )(
        features[0],
        conv_weight,
        conv_bias.reshape(width // 128, 128),
        norm_gain.reshape(width // 128, 128),
        qkv_weight,
    )
    return out[None]


def solution(mesh):
    return jax.shard_map(
        shards,
        mesh=mesh,
        in_specs=(P("dp", "seq", None), P(None, "dp", "seq"), P(), P(), P("dp", "seq")),
        out_specs=P("dp", "seq", None),
        check_vma=False,
    )
```

```python
import functools

import jax
import jax.numpy as jnp
from jax import lax
from jax.experimental import pallas as pl
from jax.experimental.pallas import tpu as pltpu
from jax.sharding import PartitionSpec as P

HK = 64
HV = 192
NH = 2
NX = 4
BF = jnp.bfloat16
F32 = jnp.float32
LAG = 3
GROUP = 128
STAGGER = 0


def kernel(
    nz, nx, ny,
    feat_in, conv_in, bias_in, gain_in, proj_in, out_ref,
    feat_ref, conv_ref, bias_ref, gain_ref, proj_ref,
    mine, feat, edge, edges, ext, wide, prev, later,
    wpack, wown, w0, w1, wflat32, wbuild, wc, pown, p0, p1, pbuild, pw,
    pool, qkv, mixed, landed,
    in_sems, send_sems, r_feat, r_edge, r_w0, r_p0, r_w1, r_p1,
    r_wa, r_wb, r_wsib, r_pool, r_kv, r_mix,
):
    dp, seq = lax.axis_index("dp"), lax.axis_index("seq")
    h, z, x = lax.div(dp, nz * nx), lax.rem(lax.div(dp, nx), nz), lax.rem(dp, nx)
    y, c = lax.div(seq, 2), lax.rem(seq, 2)
    turn = 1 - 2 * c

    def at(hh, zz, xx, yy, cc):
        return ((hh * nz + zz) * nx + xx, yy * 2 + cc)

    def round_z(offset):
        return lax.rem(z + offset + 2 * nz, nz)

    def round_x(offset):
        return lax.rem(x + offset + nx, nx)

    sibling = at(h, z, x, y, 1 - c)
    z_next, z_last = at(h, round_z(turn), x, y, c), at(h, round_z(-turn), x, y, c)
    x_next, x_last = at(h, z, round_x(turn), y, c), at(h, z, round_x(-turn), y, c)
    others_y = [lax.rem(y + d, ny) for d in (2, 1, 3)]
    others_x = [lax.rem(x + d, nx) for d in range(1, nx)]

    partners = [sibling, z_next, z_last, at(1 - h, z, x, y, 0), at(1 - h, z, x, y, 1)]
    partners += [at(h, z, x, yy, c) for yy in others_y]
    partners += [at(h, z, x, yy, 1 - c) for yy in others_y]
    partners += [at(h, z, xx, y, c) for xx in others_x]
    inputs = ((conv_in, conv_ref), (feat_in, feat_ref), (proj_in, proj_ref), (bias_in, bias_ref), (gain_in, gain_ref))
    loads = [pltpu.make_async_copy(src, dst, in_sems.at[i]) for i, (src, dst) in enumerate(inputs)]
    for load in loads:
        load.start()
    barrier = pltpu.get_barrier_semaphore()
    for device in partners:
        pl.semaphore_signal(barrier, inc=1, device_id=device, device_id_type=pl.DeviceIdType.MESH)

    for load in loads:
        load.wait()

    half_rows, lanes = mine.shape
    cin = lanes // 2
    for k in range(cin // 128):
        ext[k, : 2 * half_rows] = feat_ref[:, 128 * k : 128 * (k + 1)].astype(F32)
        mine[:, 128 * k : 128 * (k + 1)] = ext[k, pl.ds(0, half_rows, stride=2), :].astype(BF)
        mine[:, cin + 128 * k : cin + 128 * (k + 1)] = ext[k, pl.ds(1, half_rows, stride=2), :].astype(BF)
    first = mine[0:16, :].astype(F32)[0:1]
    last = mine[half_rows - 16 :, :].astype(F32)[15:16]
    strips = [row[:, 128 * k : 128 * (k + 1)] for row in (first, last) for k in range(lanes // 128)]
    spare = edge.shape[0] - len(strips)
    edge[...] = jnp.concatenate(strips + [jnp.zeros((spare, 128), F32)], axis=0).astype(BF)
    zero = jnp.zeros(edge.shape, BF)
    edges[0] = zero
    edges[ny + 1] = zero
    own = c == h
    taps, rows, cols = conv_ref.shape
    p_in, p_cols = proj_ref.shape
    wpack[...] = jnp.zeros(wpack.shape, F32)
    for t in range(taps):
        wpack[rows * t : rows * (t + 1), :cols] = conv_ref[t].astype(F32)
    wown[...] = wpack[...].astype(BF)
    pown[...] = jnp.zeros(pown.shape, BF)
    pown[:p_in, :p_cols] = proj_ref[...]

    @pl.when(own)
    def _():
        w0[c] = wown[...]
        p0[c] = pown[...]

    pl.semaphore_wait(barrier, len(partners))

    pending = []

    def copy(src, dst, recv, device, index):
        return pltpu.make_async_remote_copy(
            src_ref=src, dst_ref=dst, send_sem=send_sems.at[index], recv_sem=recv,
            device_id=device, device_id_type=pl.DeviceIdType.MESH,
        )

    def send(src, dst, recv, device, when=None):
        cp = copy(src, dst, recv, device, len(pending))
        if when is None:
            cp.start()
        else:
            pl.when(when)(cp.start)
        pending.append((cp, when))

    def arrived(dst, recv):
        copy(dst, dst, recv, sibling, 0).wait_recv()

    middle = jnp.logical_or(y == 1, y == 2)
    pass_from, pass_to = jnp.where(y == 1, 3, 0), jnp.where(y == 1, 0, 3)

    def spread(ref, dst, recv):
        for yy in others_y:
            send(ref, dst, recv.at[y], at(h, z, x, yy, c), jnp.abs(yy - y) < 3)

    def pass_on(block, recv):
        @pl.when(middle)
        def _():
            arrived(block(pass_from), recv.at[pass_from])

        send(block(pass_from), block(pass_from), recv.at[pass_from], at(h, z, x, pass_to, c), middle)

    def rest(block, recv):
        for yy in others_y:
            @pl.when(jnp.logical_not(jnp.logical_and(middle, yy == pass_from)))
            def _():
                arrived(block(yy), recv.at[yy])

    other = jnp.logical_not(own)
    send(wown, w0.at[c], r_w0.at[c], at(1 - h, z, x, y, h))
    send(wown, w0.at[c], r_w0.at[c], sibling, other)

    feat[y] = mine[...]
    spread(mine, feat.at[y], r_feat)
    for yy in others_y:
        send(edge, edges.at[1 + y], r_edge.at[y], at(h, z, x, yy, 1 - c))
    send(edge, edges.at[1 + y], r_edge.at[y], sibling)
    send(pown, p0.at[c], r_p0.at[c], at(1 - h, z, x, y, h))
    send(pown, p0.at[c], r_p0.at[c], sibling, other)

    arrived(w0.at[1 - c], r_w0.at[1 - c])

    @pl.when(other)
    def _():
        arrived(w0.at[c], r_w0.at[c])

    w1[x] = jnp.concatenate([w0[0].astype(F32)[:, :cols], w0[1].astype(F32)[:, :cols]], axis=1).astype(BF)
    for xx in others_x:
        send(w1.at[x], w1.at[x], r_w1.at[x], at(h, z, xx, y, c))

    w_rows = rows * nx
    p_rows = p_in * nx
    ups, downs = nz // 2, nz - 1 - nz // 2
    count = wc.shape[0]

    def carried(distance):
        return lax.rem(z + x + c + distance, 2) == 0

    for xx in others_x:
        arrived(w1.at[xx], r_w1.at[xx])
    for xx in range(nx):
        wflat32[...] = w1[xx].astype(F32)
        for t in range(taps):
            wbuild[t, rows * xx : rows * (xx + 1), :] = wflat32[rows * t : rows * (t + 1), :]
    for j in range(count):
        wc[j, c * nz + z] = wbuild[:, :, GROUP * j : GROUP * (j + 1)].astype(BF)

    def w_block(j, cc, zz):
        if j == count:
            return pw.at[pl.ds(pl.multiple_of((cc * nz + zz) * p_rows, 16), p_rows), :]
        return wc.at[j, cc * nz + zz]

    to_sibling = {}

    def w_start(j):
        block = w_block(j, c, z)
        send(block, block, r_wa.at[j, 0], z_next, carried(0))
        if downs:
            send(block, block, r_wb.at[j, 0], z_last, carried(0))
        send(block, block, r_wsib.at[j, 0], sibling)

    def ways(d):
        found = [(round_z(-turn * (1 + d)), r_wa, ups, z_next, x_next, 1 + d)]
        if d < downs:
            found.append((round_z(turn * (1 + d)), r_wb, downs, z_last, x_last, 1 + ups + d))
        return found

    def w_step(j, d):
        for zz, recv, steps, z_to, x_to, k in ways(d):
            block = w_block(j, c, zz)

            @pl.when(carried(1 + d))
            def _():
                arrived(block, recv.at[j, d])

            if d + 1 < steps:
                send(block, block, recv.at[j, d + 1], z_to, carried(1 + d))
        for zz, recv, steps, z_to, x_to, k in ways(d):
            block = w_block(j, c, zz)
            send(block, block, recv.at[j, d], x_to, carried(1 + d))
            cp = copy(block, block, r_wsib.at[j, k], sibling, len(pending))
            pl.when(carried(1 + d))(cp.start)
            pending.append((cp, None))
            to_sibling[j, k] = cp

    def w_finish(j, d):
        for zz, recv, steps, z_to, x_to, k in ways(d):
            @pl.when(carried(d))
            def _():
                arrived(w_block(j, c, zz), recv.at[j, d])
                to_sibling[j, k].start()

    def w_sibling(j):
        zs = [z] + [round_z(turn * (1 + d)) for d in range(ups)] + [round_z(-turn * (1 + d)) for d in range(downs)]
        for k, zz in enumerate(zs):
            arrived(w_block(j, 1 - c, zz), r_wsib.at[j, k])

    def p_join():
        arrived(p0.at[1 - c], r_p0.at[1 - c])

        @pl.when(other)
        def _():
            arrived(p0.at[c], r_p0.at[c])

        a, b = p0[0].astype(F32)[:, :p_cols], p0[1].astype(F32)[:, :p_cols]
        p1[x] = jnp.concatenate(
            [a[:, :HK], b[:, :HK], a[:, HK : 2 * HK], b[:, HK : 2 * HK], a[:, 2 * HK :], b[:, 2 * HK :]],
            axis=1,
        ).astype(BF)
        for xx in others_x:
            send(p1.at[x], p1.at[x], r_p1.at[x], at(h, z, xx, y, c))

    def p_start():
        for xx in others_x:
            arrived(p1.at[xx], r_p1.at[xx])
        for xx in range(nx):
            pbuild[p_in * xx : p_in * (xx + 1), :] = p1[xx].astype(F32)[:p_in]
        pw[pl.ds(pl.multiple_of((c * nz + z) * p_rows, 16), p_rows), :] = pbuild[...].astype(BF)
        w_start(count)

    def p_slot(k):
        if k == 0:
            p_start()
        if 0 < k <= ups:
            w_step(count, k - 1)
        if 1 < k <= ups + 1:
            w_finish(count, k - 2)

    def conv_inputs():
        for yy in others_y:
            arrived(edges.at[1 + yy], r_edge.at[yy])
        arrived(edges.at[1 + y], r_edge.at[y])
        rest(lambda yy: feat.at[yy], r_feat)
        for yy in range(ny):
            wide[8 : 8 + half_rows, :] = feat[yy].astype(F32)
            before, after = edges[yy + c].astype(F32), edges[yy + c + 1].astype(F32)
            for k in range(lanes // 128):
                wide[7:8, 128 * k : 128 * (k + 1)] = before[lanes // 128 + k : lanes // 128 + k + 1]
                wide[8 + half_rows : 9 + half_rows, 128 * k : 128 * (k + 1)] = after[k : k + 1]
            prev[yy] = wide[7 : 7 + half_rows, :].astype(BF)
            later[yy] = wide[9 : 9 + half_rows, :].astype(BF)

    for t in range(ups + 2 + STAGGER * (count - 1)):
        for j in range(count):
            k = t - STAGGER * j
            if k == 0:
                w_start(j)
            if 0 < k <= ups:
                w_step(j, k - 1)
            if 1 < k <= ups + 1:
                w_finish(j, k - 2)
        if t == 0:
            p_join()
        if t == 1:
            pass_on(lambda yy: feat.at[yy], r_feat)
        if t >= LAG and t - LAG < ups + 2:
            p_slot(t - LAG)
        if t == ups - 1:
            conv_inputs()

    cols = count * GROUP

    def dot(left, right):
        return jnp.dot(left, right, preferred_element_type=F32)

    def gelu(value, bias):
        value = value + bias
        inner = 0.7978845608028654 * (value + 0.044715 * (value * value * value))
        return value * (0.5 * (1.0 + jnp.tanh(inner)))

    def pool_part(j):
        return lambda yy: pool.at[yy, j]

    def whole(yy, rows_here=slice(None)):
        return jnp.concatenate([pool[yy, j, rows_here, :].astype(F32) for j in range(count)], axis=1)

    def conv(j):
        bias = bias_ref[pl.ds(y * (cols // 128) + j, 1), :]

        def flat(ref):
            return ref[...].reshape(ny * half_rows, lanes)

        before, now, after = flat(prev), flat(feat), flat(later)
        taken = [before[:, :cin], before[:, cin:], now[:, :cin], now[:, cin:], after[:, :cin], after[:, cin:]]
        total = None
        for t in range(taps):
            part_sum = dot(jnp.concatenate([taken[t], taken[t + 1]], axis=0), wc[j, :, t].reshape(cin, GROUP))
            total = part_sum if total is None else total + part_sum
        even, odd = total[: ny * half_rows], total[ny * half_rows :]
        pool[y, j] = jnp.maximum(gelu(even, bias), gelu(odd, bias)).astype(BF)

    left = list(range(max(ups + 2 + STAGGER * (count - 1) - LAG, 0), ups + 2))
    for j in range(count):
        w_sibling(j)
        conv(j)
        spread(pool_part(j)(y), pool_part(j)(y), r_pool.at[j])
        if left and j:
            p_slot(left.pop(0))
        if j:
            pass_on(pool_part(j - 1), r_pool.at[j - 1])
    pass_on(pool_part(count - 1), r_pool.at[count - 1])
    for k in left:
        p_slot(k)
    w_sibling(count)

    for j in range(count):
        rest(pool_part(j), r_pool.at[j])
    width = ny * cols
    total = functools.reduce(
        jnp.add, [jnp.sum(whole(yy), axis=1, keepdims=True) for yy in range(ny)]
    )
    mean = total * (1.0 / width)
    square = functools.reduce(
        jnp.add, [jnp.sum(jnp.square(whole(yy) - mean), axis=1, keepdims=True) for yy in range(ny)]
    )
    inverse = 1.0 / jnp.sqrt(square * (1.0 / width) + 1e-05)

    def gain(yy):
        k = cols // 128
        return jnp.concatenate([gain_ref[yy * k + i : yy * k + i + 1, :] for i in range(k)], axis=1)

    acc = None
    for yy in range(ny):
        normed = ((whole(yy) - mean) * inverse * gain(yy)).astype(BF)
        part = dot(normed, pw[yy * cols : (yy + 1) * cols, :])
        acc = part if acc is None else acc + part
    qkv[c] = acc.astype(BF)
    send(qkv.at[c], qkv.at[c], r_kv.at[c], sibling)

    half = half_rows * ny // 2
    lane = lax.broadcasted_iota(jnp.int32, (half, 2 * HK), 1)
    wide_lane = lax.broadcasted_iota(jnp.int32, (half, cols), 1)

    def attend(side, first):
        rows_here = pl.ds(pl.multiple_of(side * half, half), half)
        query = qkv[c, rows_here, : 2 * HK]
        none = jnp.zeros_like(query)
        both = jnp.concatenate([jnp.where(lane < HK, query, none), jnp.where(lane < HK, none, query)], axis=0)

        def score(core):
            keys = qkv[core, :, 2 * HK : 4 * HK]
            return lax.dot_general(both, keys, (((1,), (1,)), ((), ())), preferred_element_type=F32) * (HK ** -0.5)

        here = score(c)
        if first:
            arrived(qkv.at[1 - c], r_kv.at[1 - c])
        there = score(1 - c)
        top = jnp.maximum(jnp.max(here, axis=1, keepdims=True), jnp.max(there, axis=1, keepdims=True))
        here, there = jnp.exp(here - top), jnp.exp(there - top)
        inv = 1.0 / (jnp.sum(here, axis=1, keepdims=True) + jnp.sum(there, axis=1, keepdims=True))
        result = dot((here * inv).astype(BF), qkv[c, :, 4 * HK :]) + dot((there * inv).astype(BF), qkv[1 - c, :, 4 * HK :])
        attended = jnp.where(wide_lane < HV, result[:half], result[half:]).astype(BF)
        total = (whole(y, rows_here) + attended.astype(F32)).astype(BF)
        mixed[pl.ds(side * (ny // 2), ny // 2)] = total.reshape(ny // 2, half_rows, cols)

    mine_side = lax.div(y, ny // 2)
    far = (1 - mine_side) * (ny // 2)
    attend(1 - mine_side, True)
    for k in range(ny // 2):
        send(mixed.at[far + k], landed.at[y], r_mix.at[y], at(h, z, x, far + k, c))
    attend(mine_side, False)
    near = mine_side * (ny // 2) + lax.rem(y + 1, 2)
    send(mixed.at[near], landed.at[y], r_mix.at[y], at(h, z, x, near, c))
    landed[y] = mixed[y]
    writes = []
    for i, yy in enumerate([y] + others_y):
        if i:
            arrived(landed.at[yy], r_mix.at[yy])
        column = pl.multiple_of(yy * cols, 128)
        writes.append(pltpu.make_async_copy(landed.at[yy], out_ref.at[:, pl.ds(column, cols)], in_sems.at[i]))
        writes[-1].start()
    for write in writes:
        write.wait()

    for cp, when in pending:
        if when is None:
            cp.wait_send()
        else:
            pl.when(when)(cp.wait_send)


def shards(features, conv_weight, conv_bias, norm_gain, qkv_weight):
    dp, ny = lax.axis_size("dp"), lax.axis_size("seq") // 2
    nx, nz = NX, dp // (NH * NX)
    taps, rows, cols = conv_weight.shape
    cols, cin, width = 2 * cols, rows * dp, 2 * ny * cols
    half_rows = features.shape[1] // 2
    step, heads = qkv_weight.shape
    heads = 2 * heads
    positions = half_rows * ny
    dma = pltpu.SemaphoreType.DMA
    vmem = pltpu.VMEM
    ups, downs = nz // 2, nz - 1 - nz // 2
    count = cols // GROUP
    strips = pl.cdiv(2 * 2 * cin // 128, 16) * 16
    packed, p_packed = pl.cdiv(taps * rows, 16) * 16, pl.cdiv(step, 16) * 16
    sends = 4 + (ny - 1) + 1 + ny + 2 * (nx - 1) + (count + 1) * (3 * nz - 2) + count * ny + 1 + (ny - 1)
    scratch = [
        vmem(features.shape[1:], BF),
        vmem(conv_weight.shape, BF),
        vmem((width // 128, 128), F32),
        vmem((width // 128, 128), F32),
        vmem(qkv_weight.shape, BF),
        vmem((half_rows, 2 * cin), BF),
        vmem((ny, half_rows, 2 * cin), BF),
        vmem((strips, 128), BF),
        vmem((ny + 2, strips, 128), BF),
        vmem((cin // 128, 2 * half_rows + 8, 128), F32),
        vmem((half_rows + 16, 2 * cin), F32),
        vmem((ny, half_rows, 2 * cin), BF),
        vmem((ny, half_rows, 2 * cin), BF),
        vmem((packed, 256), F32),
        vmem((packed, 256), BF),
        vmem((2, packed, 256), BF),
        vmem((nx, packed, cols), BF),
        vmem((packed, cols), F32),
        vmem((taps, nx * rows, cols), F32),
        vmem((count, 2 * nz, taps, nx * rows, GROUP), BF),
        vmem((p_packed, 384), BF),
        vmem((2, p_packed, 384), BF),
        vmem((nx, p_packed, heads), BF),
        vmem((nx * step, heads), F32),
        vmem((width, heads), BF),
        vmem((ny, count, positions, GROUP), BF),
        vmem((2, positions, heads), BF),
        vmem((ny, half_rows, cols), BF),
        vmem((ny, half_rows, cols), BF),
        dma((5,)), dma((sends,)), dma((ny,)), dma((ny,)), dma((2,)), dma((2,)), dma((nx,)), dma((nx,)),
        dma((count + 1, ups)), dma((count + 1, max(downs, 1))), dma((count + 1, nz)),
        dma((count, ny)), dma((2,)), dma((ny,)),
    ]
    out = pl.pallas_call(
        functools.partial(kernel, nz, nx, ny),
        out_shape=jax.ShapeDtypeStruct((half_rows, width), BF),
        in_specs=[pl.BlockSpec(memory_space=pltpu.HBM)] * 5,
        out_specs=pl.BlockSpec(memory_space=pltpu.HBM),
        scratch_shapes=scratch,
        compiler_params=pltpu.CompilerParams(
            collective_id=0, has_side_effects=True, vmem_limit_bytes=64 * 2**20
        ),
        name="section",
    )(
        features[0],
        conv_weight,
        conv_bias.reshape(width // 128, 128),
        norm_gain.reshape(width // 128, 128),
        qkv_weight,
    )
    return out[None]


def solution(mesh):
    return jax.shard_map(
        shards,
        mesh=mesh,
        in_specs=(P("dp", "seq", None), P(None, "dp", "seq"), P(), P(), P("dp", "seq")),
        out_specs=P("dp", "seq", None),
        check_vma=False,
    )
```
